256 devices in a mesh: dp: 8 (over y, core), ctx: 32 (over x, z).
Axes of the slice: x: 4, y: 4, z: 8, core: 2. Of those that a mesh axis runs over, the one named last changes fastest.
Arguments:
- features: bfloat16 [8, 4096, 1536], P('dp', 'ctx'), may hold values from -6 to 6
- short_weight: float32 [7, 1536], replicated, may hold values from -2 to 2
- long_filter: float32 [4096, 512], P('ctx'), may hold values from -4 to 4
- skip_bias: float32 [512], replicated, may hold values from 0.5 to 1.5
- cotangent: bfloat16 [8, 4096, 512], P('dp', 'ctx'), may hold values from -6 to 6
Outputs:
- layer_out: bfloat16 [8, 4096, 512], P('dp', 'ctx')
- grad_features: bfloat16 [8, 4096, 1536], P('dp', 'ctx')
- grad_short: float32 [7, 1536], replicated
- grad_filter: float32 [4096, 512], P('ctx')
- grad_skip: float32 [512], replicated
The draws below stay inside these ranges and needn't reach their ends.
All inputs are finite; a program needn't handle non-finite values.
Results may differ from the reference program's by a relative error of at most 0.001.
Values may be sent and summed in bfloat16 or wider, within the bound.
A program may use at most 64 MiB of HBM per device.

```python
import math
import jax
import jax.numpy as jnp
from jax import lax

CH = 512
SHORT = 7
TOKENS = 4096
BATCH = 8


def draw_long_filter(key, part):
    key_mix, key_slow, key_fast, key_noise = jax.random.split(key, 4)
    slow_percent = 55
    choose_slow = jax.random.randint(key_mix, (CH,), 0, 100) < slow_percent
    slow_rate = jnp.exp(jax.random.uniform(key_slow, (CH,), jnp.float32, math.log(0.2), math.log(2.0)))
    fast_rate = jnp.exp(jax.random.uniform(key_fast, (CH,), jnp.float32, math.log(150.0), math.log(250.0)))
    rates = jnp.where(choose_slow, slow_rate, fast_rate)
    lag_axis = jnp.arange(TOKENS, dtype=jnp.float32)[:, None]
    envelope = jnp.exp(-rates[None, :] * lag_axis / TOKENS)
    amplitude = jnp.sqrt(2.0 * rates / TOKENS / (1.0 - jnp.exp(-2.0 * rates)))
    noise = jnp.clip(jax.random.normal(key_noise, (TOKENS, CH), jnp.float32), -4.0, 4.0)
    return noise * envelope * amplitude[None, :]


def shard_levels(own_key, shape, shards, smallest, top_value):
    def one(position, blocks):
        steps = jax.random.uniform(jax.random.fold_in(jax.random.fold_in(own_key, 6), position), (blocks,), jnp.float32, smallest / len(shards), top_value / len(shards))
        return jnp.repeat(jnp.exp(steps), shape[position] // blocks).reshape((-1,) + (1,) * (len(shape) - position - 1))

    level = one(*shards[0])
    for cut in shards[1:]:
        level = level * one(*cut)
    return level


def bell_draw(key, extent, scale, bound, cuts=(), kind=jnp.bfloat16):
    values = scale * jax.random.normal(key, extent, jnp.float32)
    if cuts:
        values = values * shard_levels(key, extent, cuts, -0.22, 0.18)
    return jnp.clip(values, -bound, bound).astype(kind)


def setup_inputs(seed: int = 0) -> dict:
    splits = jax.random.split(jax.random.key(seed), 6)
    return {
        "features": bell_draw(splits[0], (BATCH, TOKENS, 3 * CH), 1.0, 6.0, ((0, 8), (1, 32))),
        "short_weight": bell_draw(splits[1], (SHORT, 3 * CH), SHORT ** -0.5, 2.0, (), jnp.float32),
        "long_filter": draw_long_filter(jax.random.fold_in(splits[5], 71), 0),
        "skip_bias": jnp.clip(jax.random.uniform(splits[3], (CH,), jnp.float32, 0.5, 1.5), 0.5, 1.5),
        "cotangent": bell_draw(splits[4], (BATCH, TOKENS, CH), 1.0, 6.0, ((0, 8), (1, 32))),
    }


def reference(features, short_weight, long_filter, skip_bias, cotangent):
    source = features.astype(jnp.float32)
    length = source.shape[1]
    taps = short_weight.shape[0]
    padded = jnp.pad(source, ((0, 0), (taps - 1, 0), (0, 0)))
    mixed_feats = jnp.zeros_like(source)
    for tap_index in range(taps):
        start_row = taps - 1 - tap_index
        mixed_feats = mixed_feats + short_weight[tap_index] * padded[:, start_row:start_row + length]
    query = mixed_feats[:, :, :CH]
    key_part = mixed_feats[:, :, CH:2 * CH]
    value_part = mixed_feats[:, :, 2 * CH:]
    gated = key_part * value_part
    upstream = cotangent.astype(jnp.float32)
    dconv = upstream * query
    size_fft = 2 * length
    gated_freq = jnp.fft.rfft(gated, n=size_fft, axis=1)
    filter_freq = jnp.fft.rfft(long_filter, n=size_fft, axis=0)[None]
    dconv_freq = jnp.fft.rfft(dconv, n=size_fft, axis=1)
    long_conv = jnp.fft.irfft(gated_freq * filter_freq, n=size_fft, axis=1)[:, :length] + skip_bias * gated
    layer_out = (query * long_conv).astype(jnp.bfloat16)
    dgated = jnp.fft.irfft(jnp.conj(filter_freq) * dconv_freq, n=size_fft, axis=1)[:, :length] + skip_bias * dconv
    filter_terms = jnp.fft.irfft(jnp.conj(gated_freq) * dconv_freq, n=size_fft, axis=1)[:, :length]
    dmixed = jnp.concatenate([upstream * long_conv, dgated * value_part, dgated * key_part], axis=2)
    ahead = jnp.pad(dmixed, ((0, 0), (0, taps - 1), (0, 0)))
    grad_features = jnp.zeros_like(dmixed)
    short_rows = []
    for tap_index in range(taps):
        grad_features = grad_features + short_weight[tap_index] * ahead[:, tap_index:tap_index + length]
        start_row = taps - 1 - tap_index
        short_rows.append(lax.optimization_barrier(jnp.sum(dmixed * padded[:, start_row:start_row + length], axis=(0, 1))))
    scale = 1.0 / math.sqrt(BATCH * TOKENS)
    grad_short = jnp.stack(short_rows) * scale
    grad_filter = lax.optimization_barrier(jnp.sum(filter_terms, axis=0)) * scale
    grad_skip = lax.optimization_barrier(jnp.sum(dconv * gated, axis=(0, 1))) * scale
    return (layer_out, grad_features.astype(jnp.bfloat16), grad_short, grad_filter, grad_skip)
```

```python
import functools
import math

import jax
import jax.numpy as jnp
import ml_dtypes
import numpy as np
from jax import lax
from jax.experimental import pallas as pl
from jax.experimental.pallas import tpu as pltpu
from jax.sharding import PartitionSpec as P

MESH = pl.DeviceIdType.MESH
F32 = jnp.float32
BF16 = jnp.bfloat16

DP = 8
CTX = 32
TOK = 128
CH = 512
GRP = 16
TAPS = 7


def tables():
    index = np.arange(TOK)
    angle = 2.0 * np.pi * (np.outer(index, index) % TOK) / TOK
    cos, sin = np.cos(angle), np.sin(angle)
    forward = np.block([[cos, -sin], [sin, cos]])
    inverse = np.block([[cos, sin], [-sin, cos]]) / (CTX * TOK)
    parts = []
    for matrix in (forward, inverse):
        high = matrix.astype(np.float32).astype(ml_dtypes.bfloat16)
        low = (matrix - high.astype(np.float64)).astype(np.float32).astype(ml_dtypes.bfloat16)
        parts += [high, low]
    weights = np.stack(parts)
    inner = np.zeros((8, 8, TOK), np.float32)
    for a0 in range(8):
        for j0 in range(4):
            turn = -2.0 * np.pi * a0 * (1 + 4 * j0) / 128
            inner[a0, 2 * j0], inner[a0, 2 * j0 + 1] = np.cos(turn), np.sin(turn)
    outer = np.zeros((4, 16, TOK), np.float32)
    for j0 in range(4):
        for j1 in range(8):
            turn = -2.0 * np.pi * index * (4 * (j0 + 4 * j1) + 1) / 16384
            outer[j0, 2 * j1], outer[j0, 2 * j1 + 1] = np.cos(turn), np.sin(turn)
    return weights, inner, outer


COS1, SIN1 = math.cos(math.pi / 8), math.sin(math.pi / 8)
ROOT = math.sqrt(0.5)
COS3, SIN3 = math.cos(3 * math.pi / 8), math.sin(3 * math.pi / 8)


def cadd(x, y):
    return (x[0] + y[0], x[1] + y[1])


def csub(x, y):
    return (x[0] - y[0], x[1] - y[1])


def cmul(x, y):
    return (x[0] * y[0] - x[1] * y[1], x[0] * y[1] + x[1] * y[0])


def cmul_conj(x, y):
    return (x[0] * y[0] + x[1] * y[1], x[1] * y[0] - x[0] * y[1])


def turn(x, sign):
    return (-x[1], x[0]) if sign > 0 else (x[1], -x[0])


def dft4(x, sign):
    even, odd = cadd(x[0], x[2]), cadd(x[1], x[3])
    even1, odd1 = csub(x[0], x[2]), turn(csub(x[1], x[3]), sign)
    return [cadd(even, odd), cadd(even1, odd1), csub(even, odd), csub(even1, odd1)]


def dft8(x, sign):
    even = dft4(x[0::2], sign)
    odd = dft4(x[1::2], sign)
    first, third = odd[1], odd[3]
    if sign < 0:
        odd[1] = ((first[0] + first[1]) * ROOT, (first[1] - first[0]) * ROOT)
        odd[3] = ((third[1] - third[0]) * ROOT, (third[0] + third[1]) * -ROOT)
    else:
        odd[1] = ((first[0] - first[1]) * ROOT, (first[1] + first[0]) * ROOT)
        odd[3] = ((third[0] + third[1]) * -ROOT, (third[0] - third[1]) * ROOT)
    odd[2] = turn(odd[2], sign)
    return [cadd(even[k], odd[k]) for k in range(4)] + [csub(even[k], odd[k]) for k in range(4)]


def store_split(split_ref, slot, value):
    for half in range(2):
        high = value[half].astype(BF16)
        low = (value[half] - high.astype(F32)).astype(BF16)
        split_ref[slot, :, half * TOK : (half + 1) * TOK] = high
        split_ref[slot, :, (2 + half) * TOK : (3 + half) * TOK] = low


def product(split_ref, weights_ref, which, out_ref):
    rows = CTX * GRP
    high = split_ref[:, :, : 2 * TOK].reshape(rows, 2 * TOK)
    low = split_ref[:, :, 2 * TOK :].reshape(rows, 2 * TOK)
    dot = functools.partial(jnp.dot, preferred_element_type=F32)
    total = dot(high, weights_ref[which + 1]) + dot(low, weights_ref[which])
    total = total + dot(high, weights_ref[which])
    out_ref[...] = total.reshape(CTX, GRP, 2 * TOK)


def load_complex(ref, slot):
    return (ref[slot, :, :TOK], ref[slot, :, TOK:])


def transform(load, half_ref, split_ref, inner_ref, outer_ref, weights_ref, out_ref):
    def first(a0, carry):
        x0, x1, x2, x3 = [load(a0 + 8 * a1) for a1 in range(4)]
        t1 = (x1 * COS1, x1 * -SIN1)
        t2 = x2 * ROOT
        t3 = (x3 * COS3, x3 * -SIN3)
        even, even1 = (x0 + t2, -t2), (x0 - t2, t2)
        odd, odd1 = cadd(t1, t3), turn(csub(t1, t3), -1)
        for j0, value in enumerate([cadd(even, odd), cadd(even1, odd1), csub(even, odd), csub(even1, odd1)]):
            factor = (inner_ref[a0, 2 * j0 : 2 * j0 + 1, :], inner_ref[a0, 2 * j0 + 1 : 2 * j0 + 2, :])
            value = cmul(value, factor)
            half_ref[j0, a0, 0] = value[0]
            half_ref[j0, a0, 1] = value[1]
        return carry

    lax.fori_loop(0, 8, first, 0)

    def second(j0, carry):
        values = dft8([(half_ref[j0, a0, 0], half_ref[j0, a0, 1]) for a0 in range(8)], -1)
        for j1, value in enumerate(values):
            factor = (outer_ref[j0, 2 * j1 : 2 * j1 + 1, :], outer_ref[j0, 2 * j1 + 1 : 2 * j1 + 2, :])
            store_split(split_ref, j0 * 8 + j1, cmul(value, factor))
        return carry

    lax.fori_loop(0, 4, second, 0)
    product(split_ref, weights_ref, 0, out_ref)


def inverse(pair, emit, half_ref, split_ref, inner_ref, outer_ref, weights_ref, work_ref):
    def multiply(slot, carry):
        store_split(split_ref, slot, pair(slot))
        return carry

    lax.fori_loop(0, CTX, multiply, 0)
    product(split_ref, weights_ref, 2, work_ref)

    def second(j0, carry):
        values = []
        for j1 in range(8):
            factor = (outer_ref[j0, 2 * j1 : 2 * j1 + 1, :], outer_ref[j0, 2 * j1 + 1 : 2 * j1 + 2, :])
            values.append(cmul_conj(load_complex(work_ref, j0 * 8 + j1), factor))
        for a0, value in enumerate(dft8(values, 1)):
            half_ref[j0, a0, 0] = value[0]
            half_ref[j0, a0, 1] = value[1]
        return carry

    lax.fori_loop(0, 4, second, 0)

    def first(a0, carry):
        values = []
        for j0 in range(4):
            factor = (inner_ref[a0, 2 * j0 : 2 * j0 + 1, :], inner_ref[a0, 2 * j0 + 1 : 2 * j0 + 2, :])
            values.append(cmul_conj((half_ref[j0, a0, 0], half_ref[j0, a0, 1]), factor))
        z0, z1, z2, z3 = dft4(values, 1)
        emit(a0, z0[0])
        emit(a0 + 8, z1[0] * COS1 - z1[1] * SIN1)
        emit(a0 + 16, (z2[0] - z2[1]) * ROOT)
        emit(a0 + 24, z3[0] * COS3 - z3[1] * SIN3)
        return carry

    lax.fori_loop(0, 8, first, 0)


def kernel(
    feat_ref, cot_ref, filt_ref, short_ref, skip_ref, weights_ref, inner_ref, outer_ref,
    out_ref, gfeat_ref, gshort_ref, gfilt_ref, gskip_ref,
    send_in, recv_in, send_filt, part_filt, all_filt, send_out, recv_out, send_corr, recv_corr,
    mine_corr, part_grad, all_grad, tap_rows, tap_cols, taps, key_ref, value_ref, query_ref,
    gated_ref, dconv_ref, conv_ref, dgated_ref, half_ref, split_ref, spec_g, spec_h, spec_d, work_ref,
    sems_send, sems_recv, sem_local,
):
    dp, me = lax.axis_index("dp"), lax.axis_index("ctx")
    zed, row = lax.rem(me, 8), me // 8
    owner = zed == dp
    owner_count = jnp.where(owner, 1, 0)
    lane = lax.broadcasted_iota(jnp.int32, (GRP, TOK), 1)
    scale = 1.0 / math.sqrt(DP * CTX * TOK)

    barrier = pltpu.get_barrier_semaphore()

    def greet(dp_index, ctx_index):
        pl.semaphore_signal(barrier, inc=1, device_id={"dp": dp_index, "ctx": ctx_index}, device_id_type=MESH)

    def greet_ctx(step, carry):
        greet(dp, lax.rem(me + step, CTX))
        return carry

    lax.fori_loop(1, CTX, greet_ctx, 0)

    def greet_dp(step, carry):
        greet(lax.rem(dp + step, DP), me)
        return carry

    lax.fori_loop(1, DP, greet_dp, 0)
    for x in range(4):

        @pl.when(jnp.logical_not(jnp.logical_and(owner, row == x)))
        def _():
            greet(zed, 8 * x + dp)

    def pack(block, part, slot, base):
        columns = [base + TOK * k for k in range(4)]
        for k, start in enumerate(columns):
            tile = block[:, start : start + TOK].T
            send_in[part, 8 * k : 8 * k + 8, slot * GRP : (slot + 1) * GRP, :] = tile.reshape(8, GRP, TOK)

    for k in range(4):
        send_filt[8 * k : 8 * k + 8] = filt_ref[:, k * TOK : (k + 1) * TOK].T.reshape(8, GRP, TOK)
    pack(feat_ref, 0, 0, CH)
    pack(feat_ref, 0, 1, 2 * CH)
    pack(feat_ref, 1, 0, 0)
    pack(cot_ref, 1, 1, 0)

    pl.semaphore_wait(barrier, (CTX - 1) + (DP - 1) + 4 - owner_count)

    def remote(src, dst, index, dp_index, ctx_index):
        return pltpu.make_async_remote_copy(
            src_ref=src,
            dst_ref=dst,
            send_sem=sems_send.at[index],
            recv_sem=sems_recv.at[index],
            device_id={"dp": dp_index, "ctx": ctx_index},
            device_id_type=MESH,
        )

    def await_bytes(ref, sem):
        pltpu.make_async_copy(ref, ref, sem).wait()

    def to_ctx(make):
        def step_to(step, carry):
            make(lax.rem(me + step, CTX)).start()
            return carry

        lax.fori_loop(1, CTX, step_to, 0)

    def to_dp(make):
        def step_to(step, carry):
            make(lax.rem(dp + step, DP)).start()
            return carry

        lax.fori_loop(1, DP, step_to, 0)

    def cross(source, target_ref, index):
        for x in range(4):
            itself = jnp.logical_and(owner, row == x)

            @pl.when(jnp.logical_not(itself))
            def _():
                remote(source(x), target_ref.at[row], index, zed, 8 * x + dp).start()

            @pl.when(itself)
            def _():
                pltpu.make_async_copy(source(x), target_ref.at[row], sems_recv.at[index]).start()

    cross(lambda x: send_filt.at[8 * x + dp], part_filt, 0)
    to_ctx(lambda c: remote(send_in.at[0, c], recv_in.at[0, me], 2, dp, c))
    await_bytes(part_filt, sems_recv.at[0])
    to_dp(lambda d: remote(part_filt, all_filt.at[dp], 1, d, me))
    to_ctx(lambda c: remote(send_in.at[1, c], recv_in.at[1, me], 3, dp, c))
    all_filt[dp] = part_filt[...]
    recv_in[0, me] = send_in[0, me]
    recv_in[1, me] = send_in[1, me]

    for stream in range(3):
        for k in range(4):
            start = stream * CH + k * TOK
            tap_rows[k, 8 * stream : 8 * stream + TAPS, :] = short_ref[:, start : start + TOK]
            if stream == 0:
                tap_rows[k, TAPS : TAPS + 1, :] = skip_ref[:, k * TOK : (k + 1) * TOK]
            else:
                tap_rows[k, 8 * stream + TAPS : 8 * stream + 8, :] = jnp.zeros((1, TOK), F32)
    chosen = tap_rows[me // 8]
    tap_cols[...] = jnp.concatenate([chosen, jnp.zeros((TOK - 24, TOK), F32)], axis=0).T
    mine = tap_cols[pl.ds(pl.multiple_of(lax.rem(me, 8) * GRP, GRP), GRP), :]
    for index in range(24):
        taps[index] = jnp.broadcast_to(mine[:, index : index + 1], (GRP, TOK))

    common = (half_ref, split_ref, inner_ref, outer_ref, weights_ref)

    await_bytes(all_filt.at[pl.ds(0, DP - 1)], sems_recv.at[1])
    transform(lambda a: all_filt[lax.rem(a, 8), a // 8], *common, spec_h)

    def mix(source, before, first_tap):
        total = taps[first_tap] * source
        for tap in range(1, TAPS):
            moved = pltpu.roll(jnp.where(lane >= TOK - tap, before, source), tap, axis=1)
            total = total + taps[first_tap + tap] * moved
        return total

    await_bytes(recv_in.at[0, pl.ds(0, CTX - 1)], sems_recv.at[2])

    def mix_pair(a, carry):
        key = recv_in[0, a, :GRP, :].astype(F32)
        value = recv_in[0, a, GRP:, :].astype(F32)
        mixed_key = mix(key, carry[0], 8)
        mixed_value = mix(value, carry[1], 16)
        key_ref[a] = mixed_key
        value_ref[a] = mixed_value
        gated_ref[a] = mixed_key * mixed_value
        return (key, value)

    zero = jnp.zeros((GRP, TOK), F32)
    lax.fori_loop(0, CTX, mix_pair, (zero, zero))
    transform(lambda a: gated_ref[a], *common, spec_g)

    def emit_conv(a, value):
        conv_ref[a] = value + taps[TAPS] * gated_ref[a]

    inverse(lambda s: cmul(load_complex(spec_g, s), load_complex(spec_h, s)), emit_conv, *common, work_ref)

    await_bytes(recv_in.at[1, pl.ds(0, CTX - 1)], sems_recv.at[3])

    def mix_query(a, carry):
        query = recv_in[1, a, :GRP, :].astype(F32)
        mixed = mix(query, carry, 0)
        query_ref[a] = mixed
        dconv_ref[a] = mixed * recv_in[1, a, GRP:, :].astype(F32)
        return query

    lax.fori_loop(0, CTX, mix_query, zero)

    def back_mix(current, after, first_tap, source, sums):
        total = taps[first_tap] * current
        out_sums = [sums[0] + current * source]
        for tap in range(1, TAPS):
            moved = pltpu.roll(jnp.where(lane < tap, after, current), TOK - tap, axis=1)
            total = total + taps[first_tap + tap] * moved
            out_sums.append(sums[tap] + moved * source)
        return total, out_sums

    def back_query(step, carry):
        a = CTX - 1 - step
        after, skip_sum, sums = carry[0], carry[1], carry[2:]
        conv = conv_ref[a]
        send_out[0, a, :GRP, :] = (query_ref[a] * conv).astype(BF16)
        current = recv_in[1, a, GRP:, :].astype(F32) * conv
        total, sums = back_mix(current, after, 0, recv_in[1, a, :GRP, :].astype(F32), sums)
        send_out[0, a, GRP:, :] = total.astype(BF16)
        return (current, skip_sum + dconv_ref[a] * gated_ref[a], *sums)

    sums_query = lax.fori_loop(0, CTX, back_query, (zero,) * 9)[1:]
    to_ctx(lambda c: remote(send_out.at[0, c], recv_out.at[0, me], 4, dp, c))
    recv_out[0, me] = send_out[0, me]

    def collect(start, columns, small):
        for offset, column in enumerate(columns):
            small = jnp.where(lane == start + offset, jnp.sum(column, axis=1, keepdims=True), small)
        return small

    small = collect(TAPS, sums_query[:1], zero)
    small = collect(0, sums_query[1:], small)

    transform(lambda a: dconv_ref[a], *common, spec_d)

    def emit_back(a, value):
        dgated_ref[a] = value + taps[TAPS] * dconv_ref[a]

    inverse(lambda s: cmul_conj(load_complex(spec_d, s), load_complex(spec_h, s)), emit_back, *common, work_ref)

    for slot, (partner, first_tap) in enumerate([(value_ref, 8), (key_ref, 16)]):

        def back_pair(step, carry, slot=slot, partner=partner, first_tap=first_tap):
            a = CTX - 1 - step
            rows = slice(slot * GRP, (slot + 1) * GRP)
            current = dgated_ref[a] * partner[a]
            total, sums = back_mix(current, carry[0], first_tap, recv_in[0, a, rows, :].astype(F32), carry[1:])
            send_out[1, a, rows, :] = total.astype(BF16)
            return (current, *sums)

        small = collect(first_tap, lax.fori_loop(0, CTX, back_pair, (zero,) * 8)[1:], small)

    to_ctx(lambda c: remote(send_out.at[1, c], recv_out.at[1, me], 5, dp, c))
    recv_out[1, me] = send_out[1, me]

    def emit_corr(a, value):
        send_corr[lax.rem(a, 8), a // 8] = value * scale

    inverse(lambda s: cmul_conj(load_complex(spec_d, s), load_complex(spec_g, s)), emit_corr, *common, work_ref)
    for member in range(DP):
        send_corr[member, 4] = small * scale
    to_dp(lambda d: remote(send_corr.at[d], recv_corr.at[dp], 6, d, me))
    recv_corr[dp] = send_corr[dp]

    def unpack(part, slot, target_ref, base):
        for k in range(4):
            tile = recv_out[part, 8 * k : 8 * k + 8, slot * GRP : (slot + 1) * GRP, :].reshape(TOK, TOK)
            target_ref[:, base + k * TOK : base + (k + 1) * TOK] = tile.T

    await_bytes(recv_corr.at[pl.ds(0, DP - 1)], sems_recv.at[6])
    total = recv_corr[0]
    for member in range(1, DP):
        total = total + recv_corr[member]
    mine_corr[...] = total

    cross(lambda x: mine_corr.at[x], part_grad, 7)

    @pl.when(owner)
    def _():
        pltpu.make_async_copy(mine_corr.at[4], part_grad.at[4 + row], sems_recv.at[7]).start()
        to_ctx(lambda c: remote(mine_corr.at[4], part_grad.at[4 + row], 8, dp, c))

    @pl.when(owner)
    def _():
        await_bytes(part_grad.at[pl.ds(0, 5)], sems_recv.at[7])
        await_bytes(part_grad.at[pl.ds(0, 3)], sems_recv.at[8])

    @pl.when(jnp.logical_not(owner))
    def _():
        await_bytes(part_grad.at[pl.ds(0, 4)], sems_recv.at[7])
        await_bytes(part_grad.at[pl.ds(0, 4)], sems_recv.at[8])

    to_dp(lambda d: remote(part_grad, all_grad.at[dp], 9, d, me))
    all_grad[dp] = part_grad[...]

    await_bytes(recv_out.at[0, pl.ds(0, CTX - 1)], sems_recv.at[4])
    unpack(0, 0, out_ref, 0)
    unpack(0, 1, gfeat_ref, 0)
    await_bytes(recv_out.at[1, pl.ds(0, CTX - 1)], sems_recv.at[5])
    unpack(1, 0, gfeat_ref, CH)
    unpack(1, 1, gfeat_ref, 2 * CH)

    await_bytes(all_grad.at[pl.ds(0, DP - 1)], sems_recv.at[9])
    for x in range(4):
        columns = slice(x * TOK, (x + 1) * TOK)
        gfilt_ref[:, columns] = all_grad[:, x].reshape(TOK, TOK).T
        rows = all_grad[:, 4 + x].reshape(TOK, TOK).T
        gskip_ref[:, columns] = rows[TAPS : TAPS + 1, :]
        for stream in range(3):
            gshort_ref[:, stream * CH + x * TOK : stream * CH + (x + 1) * TOK] = rows[8 * stream : 8 * stream + TAPS, :]

    @pl.when(owner)
    def _():
        await_bytes(send_filt.at[pl.ds(0, 3)], sems_send.at[0])
        await_bytes(mine_corr.at[pl.ds(0, 3)], sems_send.at[7])
        await_bytes(send_filt.at[pl.ds(0, CTX - 1)], sems_send.at[8])

    @pl.when(jnp.logical_not(owner))
    def _():
        await_bytes(send_filt.at[pl.ds(0, 4)], sems_send.at[0])
        await_bytes(mine_corr.at[pl.ds(0, 4)], sems_send.at[7])

    await_bytes(all_filt.at[pl.ds(0, DP - 1)], sems_send.at[1])
    for part in range(2):
        await_bytes(send_in.at[part, pl.ds(0, CTX - 1)], sems_send.at[2 + part])
        await_bytes(send_out.at[part, pl.ds(0, CTX - 1)], sems_send.at[4 + part])
    await_bytes(send_corr.at[pl.ds(0, DP - 1)], sems_send.at[6])
    await_bytes(all_grad.at[pl.ds(0, DP - 1)], sems_send.at[9])


def per_device(features, short_weight, long_filter, skip_bias, cotangent):
    weights, inner, outer = tables()
    vmem = pl.BlockSpec(memory_space=pltpu.VMEM)
    block = (CTX, GRP, TOK)
    out, gfeat, gshort, gfilt, gskip = pl.pallas_call(
        kernel,
        out_shape=(
            jax.ShapeDtypeStruct((TOK, CH), BF16),
            jax.ShapeDtypeStruct((TOK, 3 * CH), BF16),
            jax.ShapeDtypeStruct((TAPS, 3 * CH), F32),
            jax.ShapeDtypeStruct((TOK, CH), F32),
            jax.ShapeDtypeStruct((1, CH), F32),
        ),
        in_specs=[vmem] * 8,
        out_specs=(vmem,) * 5,
        scratch_shapes=[
            pltpu.VMEM((2, CTX, 2 * GRP, TOK), BF16),
            pltpu.VMEM((2, CTX, 2 * GRP, TOK), BF16),
            pltpu.VMEM(block, F32),
            pltpu.VMEM((4, GRP, TOK), F32),
            pltpu.VMEM((DP, 4, GRP, TOK), F32),
            pltpu.VMEM((2, CTX, 2 * GRP, TOK), BF16),
            pltpu.VMEM((2, CTX, 2 * GRP, TOK), BF16),
            pltpu.VMEM((DP, 5, GRP, TOK), F32),
            pltpu.VMEM((DP, 5, GRP, TOK), F32),
            pltpu.VMEM((5, GRP, TOK), F32),
            pltpu.VMEM((8, GRP, TOK), F32),
            pltpu.VMEM((DP, 8, GRP, TOK), F32),
            pltpu.VMEM((4, 24, TOK), F32),
            pltpu.VMEM((TOK, TOK), F32),
            pltpu.VMEM((24, GRP, TOK), F32),
            pltpu.VMEM(block, F32),
            pltpu.VMEM(block, F32),
            pltpu.VMEM(block, F32),
            pltpu.VMEM(block, F32),
            pltpu.VMEM(block, F32),
            pltpu.VMEM(block, F32),
            pltpu.VMEM(block, F32),
            pltpu.VMEM((4, 8, 2, GRP, TOK), F32),
            pltpu.VMEM((CTX, GRP, 4 * TOK), BF16),
            pltpu.VMEM((CTX, GRP, 2 * TOK), F32),
            pltpu.VMEM((CTX, GRP, 2 * TOK), F32),
            pltpu.VMEM((CTX, GRP, 2 * TOK), F32),
            pltpu.VMEM((CTX, GRP, 2 * TOK), F32),
            pltpu.SemaphoreType.DMA((10,)),
            pltpu.SemaphoreType.DMA((10,)),
            pltpu.SemaphoreType.DMA,
        ],
        compiler_params=pltpu.CompilerParams(
            collective_id=0, has_side_effects=True, vmem_limit_bytes=40 << 20
        ),
        name="hyena",
    )(
        features[0], cotangent[0], long_filter, short_weight, skip_bias.reshape(1, CH),
        jnp.asarray(weights), jnp.asarray(inner), jnp.asarray(outer),
    )
    return (out[None], gfeat[None], gshort, gfilt, gskip.reshape(CH))


def solution(mesh):
    return jax.shard_map(
        per_device,
        mesh=mesh,
        in_specs=(P("dp", "ctx", None), P(), P("ctx", None), P(), P("dp", "ctx", None)),
        out_specs=(P("dp", "ctx", None), P("dp", "ctx", None), P(), P("ctx", None), P()),
        check_vma=False,
    )
```

```python
import functools
import math

import jax
import jax.numpy as jnp
import ml_dtypes
import numpy as np
from jax import lax
from jax.experimental import pallas as pl
from jax.experimental.pallas import tpu as pltpu
from jax.sharding import PartitionSpec as P

MESH = pl.DeviceIdType.MESH
F32 = jnp.float32
BF16 = jnp.bfloat16

DP = 8
CTX = 32
TOK = 128
CH = 512
GRP = 16
TAPS = 7


def tables():
    index = np.arange(TOK)
    angle = 2.0 * np.pi * (np.outer(index, index) % TOK) / TOK
    cos, sin = np.cos(angle), np.sin(angle)
    forward = np.block([[cos, -sin], [sin, cos]])
    inverse = np.block([[cos, sin], [-sin, cos]]) / (CTX * TOK)
    parts = []
    for matrix in (forward, inverse):
        high = matrix.astype(np.float32).astype(ml_dtypes.bfloat16)
        low = (matrix - high.astype(np.float64)).astype(np.float32).astype(ml_dtypes.bfloat16)
        parts += [high, low]
    weights = np.stack(parts)
    inner = np.zeros((8, 8, TOK), np.float32)
    for a0 in range(8):
        for j0 in range(4):
            turn = -2.0 * np.pi * a0 * (1 + 4 * j0) / 128
            inner[a0, 2 * j0], inner[a0, 2 * j0 + 1] = np.cos(turn), np.sin(turn)
    outer = np.zeros((4, 16, TOK), np.float32)
    for j0 in range(4):
        for j1 in range(8):
            turn = -2.0 * np.pi * index * (4 * (j0 + 4 * j1) + 1) / 16384
            outer[j0, 2 * j1], outer[j0, 2 * j1 + 1] = np.cos(turn), np.sin(turn)
    return weights, inner, outer


COS1, SIN1 = math.cos(math.pi / 8), math.sin(math.pi / 8)
ROOT = math.sqrt(0.5)
COS3, SIN3 = math.cos(3 * math.pi / 8), math.sin(3 * math.pi / 8)


def cadd(x, y):
    return (x[0] + y[0], x[1] + y[1])


def csub(x, y):
    return (x[0] - y[0], x[1] - y[1])


def cmul(x, y):
    return (x[0] * y[0] - x[1] * y[1], x[0] * y[1] + x[1] * y[0])


def cmul_conj(x, y):
    return (x[0] * y[0] + x[1] * y[1], x[1] * y[0] - x[0] * y[1])


def turn(x, sign):
    return (-x[1], x[0]) if sign > 0 else (x[1], -x[0])


def dft4(x, sign):
    even, odd = cadd(x[0], x[2]), cadd(x[1], x[3])
    even1, odd1 = csub(x[0], x[2]), turn(csub(x[1], x[3]), sign)
    return [cadd(even, odd), cadd(even1, odd1), csub(even, odd), csub(even1, odd1)]


def dft8(x, sign):
    even = dft4(x[0::2], sign)
    odd = dft4(x[1::2], sign)
    first, third = odd[1], odd[3]
    if sign < 0:
        odd[1] = ((first[0] + first[1]) * ROOT, (first[1] - first[0]) * ROOT)
        odd[3] = ((third[1] - third[0]) * ROOT, (third[0] + third[1]) * -ROOT)
    else:
        odd[1] = ((first[0] - first[1]) * ROOT, (first[1] + first[0]) * ROOT)
        odd[3] = ((third[0] + third[1]) * -ROOT, (third[0] - third[1]) * ROOT)
    odd[2] = turn(odd[2], sign)
    return [cadd(even[k], odd[k]) for k in range(4)] + [csub(even[k], odd[k]) for k in range(4)]


def store_split(split_ref, slot, value):
    for half in range(2):
        high = value[half].astype(BF16)
        low = (value[half] - high.astype(F32)).astype(BF16)
        split_ref[slot, :, half * TOK : (half + 1) * TOK] = high
        split_ref[slot, :, (2 + half) * TOK : (3 + half) * TOK] = low


def product(split_ref, weights_ref, which, out_ref):
    rows = CTX * GRP
    high = split_ref[:, :, : 2 * TOK].reshape(rows, 2 * TOK)
    low = split_ref[:, :, 2 * TOK :].reshape(rows, 2 * TOK)
    dot = functools.partial(jnp.dot, preferred_element_type=F32)
    total = dot(high, weights_ref[which + 1]) + dot(low, weights_ref[which])
    total = total + dot(high, weights_ref[which])
    out_ref[...] = total.reshape(CTX, GRP, 2 * TOK)


def load_complex(ref, slot):
    return (ref[slot, :, :TOK], ref[slot, :, TOK:])


def transform(load, half_ref, split_ref, inner_ref, outer_ref, weights_ref, out_ref):
    def first(a0, carry):
        x0, x1, x2, x3 = [load(a0 + 8 * a1) for a1 in range(4)]
        t1 = (x1 * COS1, x1 * -SIN1)
        t2 = x2 * ROOT
        t3 = (x3 * COS3, x3 * -SIN3)
        even, even1 = (x0 + t2, -t2), (x0 - t2, t2)
        odd, odd1 = cadd(t1, t3), turn(csub(t1, t3), -1)
        for j0, value in enumerate([cadd(even, odd), cadd(even1, odd1), csub(even, odd), csub(even1, odd1)]):
            factor = (inner_ref[a0, 2 * j0 : 2 * j0 + 1, :], inner_ref[a0, 2 * j0 + 1 : 2 * j0 + 2, :])
            value = cmul(value, factor)
            half_ref[j0, a0, 0] = value[0]
            half_ref[j0, a0, 1] = value[1]
        return carry

    lax.fori_loop(0, 8, first, 0)

    def second(j0, carry):
        values = dft8([(half_ref[j0, a0, 0], half_ref[j0, a0, 1]) for a0 in range(8)], -1)
        for j1, value in enumerate(values):
            factor = (outer_ref[j0, 2 * j1 : 2 * j1 + 1, :], outer_ref[j0, 2 * j1 + 1 : 2 * j1 + 2, :])
            store_split(split_ref, j0 * 8 + j1, cmul(value, factor))
        return carry

    lax.fori_loop(0, 4, second, 0)
    product(split_ref, weights_ref, 0, out_ref)


def inverse(pair, emit, half_ref, split_ref, inner_ref, outer_ref, weights_ref, work_ref):
    def multiply(slot, carry):
        store_split(split_ref, slot, pair(slot))
        return carry

    lax.fori_loop(0, CTX, multiply, 0)
    product(split_ref, weights_ref, 2, work_ref)

    def second(j0, carry):
        values = []
        for j1 in range(8):
            factor = (outer_ref[j0, 2 * j1 : 2 * j1 + 1, :], outer_ref[j0, 2 * j1 + 1 : 2 * j1 + 2, :])
            values.append(cmul_conj(load_complex(work_ref, j0 * 8 + j1), factor))
        for a0, value in enumerate(dft8(values, 1)):
            half_ref[j0, a0, 0] = value[0]
            half_ref[j0, a0, 1] = value[1]
        return carry

    lax.fori_loop(0, 4, second, 0)

    def first(a0, carry):
        values = []
        for j0 in range(4):
            factor = (inner_ref[a0, 2 * j0 : 2 * j0 + 1, :], inner_ref[a0, 2 * j0 + 1 : 2 * j0 + 2, :])
            values.append(cmul_conj((half_ref[j0, a0, 0], half_ref[j0, a0, 1]), factor))
        z0, z1, z2, z3 = dft4(values, 1)
        emit(a0, z0[0])
        emit(a0 + 8, z1[0] * COS1 - z1[1] * SIN1)
        emit(a0 + 16, (z2[0] - z2[1]) * ROOT)
        emit(a0 + 24, z3[0] * COS3 - z3[1] * SIN3)
        return carry

    lax.fori_loop(0, 8, first, 0)


def kernel(
    feat_hbm, cot_hbm, filt_hbm, short_hbm, skip_hbm, weights_hbm, inner_hbm, outer_hbm,
    out_ref, gfeat_ref, gshort_ref, gfilt_ref, gskip_ref,
    feat_ref, cot_ref, filt_ref, short_ref, skip_ref, weights_ref, inner_ref, outer_ref,
    send_in, recv_in, send_filt, part_filt, all_filt, send_out, recv_out, send_corr, recv_corr,
    mine_corr, part_grad, all_grad, tap_rows, tap_cols, taps, key_ref, value_ref, query_ref,
    gated_ref, dconv_ref, conv_ref, dgated_ref, half_ref, split_ref, spec_g, spec_h, spec_d, work_ref,
    small_send, small_dp, small_zed, small_row, sems_send, sems_recv, sems_load,
):
    loads = [
        pltpu.make_async_copy(source, target, sems_load.at[index])
        for index, (source, target) in enumerate(
            [
                (filt_hbm, filt_ref), (feat_hbm, feat_ref), (cot_hbm, cot_ref), (short_hbm, short_ref),
                (skip_hbm, skip_ref), (inner_hbm, inner_ref), (outer_hbm, outer_ref), (weights_hbm, weights_ref),
            ]
        )
    ]
    for load in loads:
        load.start()
    dp, me = lax.axis_index("dp"), lax.axis_index("ctx")
    zed, row = lax.rem(me, 8), me // 8
    owner = zed == dp
    owner_count = jnp.where(owner, 1, 0)
    lane = lax.broadcasted_iota(jnp.int32, (GRP, TOK), 1)
    scale = 1.0 / math.sqrt(DP * CTX * TOK)

    barrier = pltpu.get_barrier_semaphore()

    def greet(dp_index, ctx_index):
        pl.semaphore_signal(barrier, inc=1, device_id={"dp": dp_index, "ctx": ctx_index}, device_id_type=MESH)

    def greet_ctx(step, carry):
        greet(dp, lax.rem(me + step, CTX))
        return carry

    lax.fori_loop(1, CTX, greet_ctx, 0)

    def greet_dp(step, carry):
        greet(lax.rem(dp + step, DP), me)
        return carry

    lax.fori_loop(1, DP, greet_dp, 0)
    for x in range(4):

        @pl.when(jnp.logical_not(jnp.logical_and(owner, row == x)))
        def _():
            greet(zed, 8 * x + dp)

    def pack(block, part, slot, base):
        columns = [base + TOK * k for k in range(4)]
        for k, start in enumerate(columns):
            tile = block[:, start : start + TOK].T
            send_in[part, 8 * k : 8 * k + 8, slot * GRP : (slot + 1) * GRP, :] = tile.reshape(8, GRP, TOK)

    loads[0].wait()
    for k in range(4):
        send_filt[8 * k : 8 * k + 8] = filt_ref[:, k * TOK : (k + 1) * TOK].T.reshape(8, GRP, TOK)
    loads[1].wait()
    pack(feat_ref, 0, 0, CH)
    pack(feat_ref, 0, 1, 2 * CH)
    pack(feat_ref, 1, 0, 0)
    loads[2].wait()
    pack(cot_ref, 1, 1, 0)

    pl.semaphore_wait(barrier, (CTX - 1) + (DP - 1) + 4 - owner_count)

    def remote(src, dst, index, dp_index, ctx_index):
        return pltpu.make_async_remote_copy(
            src_ref=src,
            dst_ref=dst,
            send_sem=sems_send.at[index],
            recv_sem=sems_recv.at[index],
            device_id={"dp": dp_index, "ctx": ctx_index},
            device_id_type=MESH,
        )

    def await_bytes(ref, sem):
        pltpu.make_async_copy(ref, ref, sem).wait()

    def to_ctx(make):
        def step_to(step, carry):
            make(lax.rem(me + step, CTX)).start()
            return carry

        lax.fori_loop(1, CTX, step_to, 0)

    def to_dp(make):
        def step_to(step, carry):
            make(lax.rem(dp + step, DP)).start()
            return carry

        lax.fori_loop(1, DP, step_to, 0)

    def cross(source, target_ref, index):
        for x in range(4):
            itself = jnp.logical_and(owner, row == x)

            @pl.when(jnp.logical_not(itself))
            def _():
                remote(source(x), target_ref.at[row], index, zed, 8 * x + dp).start()

            @pl.when(itself)
            def _():
                pltpu.make_async_copy(source(x), target_ref.at[row], sems_recv.at[index]).start()

    cross(lambda x: send_filt.at[8 * x + dp], part_filt, 0)
    to_ctx(lambda c: remote(send_in.at[0, c], recv_in.at[0, me], 2, dp, c))
    await_bytes(part_filt, sems_recv.at[0])
    to_dp(lambda d: remote(part_filt, all_filt.at[dp], 1, d, me))
    to_ctx(lambda c: remote(send_in.at[1, c], recv_in.at[1, me], 3, dp, c))
    all_filt[dp] = part_filt[...]
    recv_in[0, me] = send_in[0, me]
    recv_in[1, me] = send_in[1, me]

    for load in loads[3:]:
        load.wait()

    for stream in range(3):
        for k in range(4):
            start = stream * CH + k * TOK
            tap_rows[k, 8 * stream : 8 * stream + TAPS, :] = short_ref[:, start : start + TOK]
            if stream == 0:
                tap_rows[k, TAPS : TAPS + 1, :] = skip_ref[:, k * TOK : (k + 1) * TOK]
            else:
                tap_rows[k, 8 * stream + TAPS : 8 * stream + 8, :] = jnp.zeros((1, TOK), F32)
    chosen = tap_rows[me // 8]
    tap_cols[...] = jnp.concatenate([chosen, jnp.zeros((TOK - 24, TOK), F32)], axis=0).T
    mine = tap_cols[pl.ds(pl.multiple_of(lax.rem(me, 8) * GRP, GRP), GRP), :]
    for index in range(24):
        taps[index] = jnp.broadcast_to(mine[:, index : index + 1], (GRP, TOK))

    common = (half_ref, split_ref, inner_ref, outer_ref, weights_ref)

    await_bytes(all_filt.at[pl.ds(0, DP - 1)], sems_recv.at[1])
    transform(lambda a: all_filt[lax.rem(a, 8), a // 8], *common, spec_h)

    def mix(source, before, first_tap):
        total = taps[first_tap] * source
        for tap in range(1, TAPS):
            moved = pltpu.roll(jnp.where(lane >= TOK - tap, before, source), tap, axis=1)
            total = total + taps[first_tap + tap] * moved
        return total

    await_bytes(recv_in.at[0, pl.ds(0, CTX - 1)], sems_recv.at[2])

    def mix_pair(a, carry):
        key = recv_in[0, a, :GRP, :].astype(F32)
        value = recv_in[0, a, GRP:, :].astype(F32)
        mixed_key = mix(key, carry[0], 8)
        mixed_value = mix(value, carry[1], 16)
        key_ref[a] = mixed_key
        value_ref[a] = mixed_value
        gated_ref[a] = mixed_key * mixed_value
        return (key, value)

    zero = jnp.zeros((GRP, TOK), F32)
    lax.fori_loop(0, CTX, mix_pair, (zero, zero), unroll=4)
    transform(lambda a: gated_ref[a], *common, spec_g)

    def emit_conv(a, value):
        conv_ref[a] = value + taps[TAPS] * gated_ref[a]

    inverse(lambda s: cmul(load_complex(spec_g, s), load_complex(spec_h, s)), emit_conv, *common, work_ref)

    await_bytes(recv_in.at[1, pl.ds(0, CTX - 1)], sems_recv.at[3])

    def mix_query(a, carry):
        query = recv_in[1, a, :GRP, :].astype(F32)
        mixed = mix(query, carry, 0)
        query_ref[a] = mixed
        dconv_ref[a] = mixed * recv_in[1, a, GRP:, :].astype(F32)
        return query

    lax.fori_loop(0, CTX, mix_query, zero, unroll=4)

    def back_mix(current, after, first_tap, source, sums):
        total = taps[first_tap] * current
        out_sums = [sums[0] + current * source]
        for tap in range(1, TAPS):
            moved = pltpu.roll(jnp.where(lane < tap, after, current), TOK - tap, axis=1)
            total = total + taps[first_tap + tap] * moved
            out_sums.append(sums[tap] + moved * source)
        return total, out_sums

    def back_query(step, carry):
        a = CTX - 1 - step
        after, skip_sum, sums = carry[0], carry[1], carry[2:]
        conv = conv_ref[a]
        send_out[0, a, :GRP, :] = (query_ref[a] * conv).astype(BF16)
        current = recv_in[1, a, GRP:, :].astype(F32) * conv
        total, sums = back_mix(current, after, 0, recv_in[1, a, :GRP, :].astype(F32), sums)
        send_out[0, a, GRP:, :] = total.astype(BF16)
        return (current, skip_sum + dconv_ref[a] * gated_ref[a], *sums)

    sums_query = lax.fori_loop(0, CTX, back_query, (zero,) * 9, unroll=4)[1:]
    to_ctx(lambda c: remote(send_out.at[0, c], recv_out.at[0, me], 4, dp, c))
    recv_out[0, me] = send_out[0, me]

    def collect(start, columns, small):
        for offset, column in enumerate(columns):
            small = jnp.where(lane == start + offset, jnp.sum(column, axis=1, keepdims=True), small)
        return small

    small = collect(TAPS, sums_query[:1], zero)
    small = collect(0, sums_query[1:], small)

    transform(lambda a: dconv_ref[a], *common, spec_d)

    def emit_back(a, value):
        dgated_ref[a] = value + taps[TAPS] * dconv_ref[a]

    inverse(lambda s: cmul_conj(load_complex(spec_d, s), load_complex(spec_h, s)), emit_back, *common, work_ref)

    def emit_corr(a, value):
        send_corr[lax.rem(a, 8), a // 8] = value * scale

    inverse(lambda s: cmul_conj(load_complex(spec_d, s), load_complex(spec_g, s)), emit_corr, *common, work_ref)
    to_dp(lambda d: remote(send_corr.at[d], recv_corr.at[dp], 6, d, me))
    recv_corr[dp] = send_corr[dp]

    for slot, (partner, first_tap) in enumerate([(value_ref, 8), (key_ref, 16)]):

        def back_pair(step, carry, slot=slot, partner=partner, first_tap=first_tap):
            a = CTX - 1 - step
            rows = slice(slot * GRP, (slot + 1) * GRP)
            current = dgated_ref[a] * partner[a]
            total, sums = back_mix(current, carry[0], first_tap, recv_in[0, a, rows, :].astype(F32), carry[1:])
            send_out[1, a, rows, :] = total.astype(BF16)
            return (current, *sums)

        small = collect(first_tap, lax.fori_loop(0, CTX, back_pair, (zero,) * 8, unroll=4)[1:], small)

    tap_cols[...] = jnp.zeros((TOK, TOK), F32)
    tap_cols[pl.ds(pl.multiple_of(zed * GRP, GRP), GRP), :] = small * scale
    small_send[0] = tap_cols[...].T[:24, :]
    small_dp[dp] = small_send[0]
    to_dp(lambda d: remote(small_send.at[0], small_dp.at[dp], 8, d, me))
    to_ctx(lambda c: remote(send_out.at[1, c], recv_out.at[1, me], 5, dp, c))
    recv_out[1, me] = send_out[1, me]

    def unpack(part, slot, target_ref, base):
        for k in range(4):
            tile = recv_out[part, 8 * k : 8 * k + 8, slot * GRP : (slot + 1) * GRP, :].reshape(TOK, TOK)
            target_ref[:, base + k * TOK : base + (k + 1) * TOK] = tile.T

    def summed(ref):
        total = ref[0]
        for index in range(1, 8):
            total = total + ref[index]
        return total

    await_bytes(recv_corr.at[pl.ds(0, DP - 1)], sems_recv.at[6])
    mine_corr[...] = summed(recv_corr)
    cross(lambda x: mine_corr.at[x], part_grad, 7)

    await_bytes(small_dp.at[pl.ds(0, DP - 1)], sems_recv.at[8])
    small_send[1] = summed(small_dp)
    small_zed[zed] = small_send[1]
    for step in range(1, 8):
        remote(small_send.at[1], small_zed.at[zed], 10, dp, 8 * row + lax.rem(zed + step, 8)).start()

    await_bytes(part_grad, sems_recv.at[7])
    to_dp(lambda d: remote(part_grad, all_grad.at[dp], 9, d, me))
    all_grad[dp] = part_grad[...]

    await_bytes(small_zed.at[pl.ds(0, 7)], sems_recv.at[10])
    small_send[2] = summed(small_zed)
    small_row[row] = small_send[2]
    for step in range(1, 4):
        remote(small_send.at[2], small_row.at[row], 11, dp, 8 * lax.rem(row + step, 4) + zed).start()

    await_bytes(recv_out.at[0, pl.ds(0, CTX - 1)], sems_recv.at[4])
    unpack(0, 0, out_ref, 0)
    unpack(0, 1, gfeat_ref, 0)
    await_bytes(small_row.at[pl.ds(0, 3)], sems_recv.at[11])
    for x in range(4):
        gskip_ref[:, x * TOK : (x + 1) * TOK] = small_row[x, TAPS : TAPS + 1, :]
        for stream in range(3):
            columns = slice(stream * CH + x * TOK, stream * CH + (x + 1) * TOK)
            gshort_ref[:, columns] = small_row[x, 8 * stream : 8 * stream + TAPS, :]
    await_bytes(recv_out.at[1, pl.ds(0, CTX - 1)], sems_recv.at[5])
    unpack(1, 0, gfeat_ref, CH)
    unpack(1, 1, gfeat_ref, 2 * CH)
    await_bytes(all_grad.at[pl.ds(0, DP - 1)], sems_recv.at[9])
    for x in range(4):
        gfilt_ref[:, x * TOK : (x + 1) * TOK] = all_grad[:, x].reshape(TOK, TOK).T

    @pl.when(owner)
    def _():
        await_bytes(send_filt.at[pl.ds(0, 3)], sems_send.at[0])
        await_bytes(mine_corr.at[pl.ds(0, 3)], sems_send.at[7])

    @pl.when(jnp.logical_not(owner))
    def _():
        await_bytes(send_filt.at[pl.ds(0, 4)], sems_send.at[0])
        await_bytes(mine_corr.at[pl.ds(0, 4)], sems_send.at[7])

    await_bytes(all_filt.at[pl.ds(0, DP - 1)], sems_send.at[1])
    for part in range(2):
        await_bytes(send_in.at[part, pl.ds(0, CTX - 1)], sems_send.at[2 + part])
        await_bytes(send_out.at[part, pl.ds(0, CTX - 1)], sems_send.at[4 + part])
    await_bytes(send_corr.at[pl.ds(0, DP - 1)], sems_send.at[6])
    await_bytes(small_dp.at[pl.ds(0, DP - 1)], sems_send.at[8])
    await_bytes(all_grad.at[pl.ds(0, DP - 1)], sems_send.at[9])
    await_bytes(small_zed.at[pl.ds(0, 7)], sems_send.at[10])
    await_bytes(small_row.at[pl.ds(0, 3)], sems_send.at[11])


def deliver(*refs):
    sources, targets, sems = refs[:5], refs[5:10], refs[10]
    copies = [pltpu.make_async_copy(sources[index], targets[index], sems.at[index]) for index in range(5)]
    for copy in copies:
        copy.start()
    for copy in copies:
        copy.wait()


def per_device(features, short_weight, long_filter, skip_bias, cotangent):
    weights, inner, outer = tables()
    hbm = pl.BlockSpec(memory_space=pltpu.HBM)
    vmem = pl.BlockSpec(memory_space=pltpu.VMEM)
    block = (CTX, GRP, TOK)
    shapes = (
        jax.ShapeDtypeStruct((TOK, CH), BF16),
        jax.ShapeDtypeStruct((TOK, 3 * CH), BF16),
        jax.ShapeDtypeStruct((TAPS, 3 * CH), F32),
        jax.ShapeDtypeStruct((TOK, CH), F32),
        jax.ShapeDtypeStruct((1, CH), F32),
    )
    operands = [
        features[0], cotangent[0], long_filter, short_weight, skip_bias.reshape(1, CH),
        jnp.asarray(weights), jnp.asarray(inner), jnp.asarray(outer),
    ]
    operands = [pltpu.with_memory_space_constraint(operand, pltpu.HBM) for operand in operands]
    results = pl.pallas_call(
        kernel,
        out_shape=shapes,
        in_specs=[hbm] * 8,
        out_specs=(vmem,) * 5,
        scratch_shapes=[
            pltpu.VMEM((TOK, 3 * CH), BF16),
            pltpu.VMEM((TOK, CH), BF16),
            pltpu.VMEM((TOK, CH), F32),
            pltpu.VMEM((TAPS, 3 * CH), F32),
            pltpu.VMEM((1, CH), F32),
            pltpu.VMEM(weights.shape, BF16),
            pltpu.VMEM(inner.shape, F32),
            pltpu.VMEM(outer.shape, F32),
            pltpu.VMEM((2, CTX, 2 * GRP, TOK), BF16),
            pltpu.VMEM((2, CTX, 2 * GRP, TOK), BF16),
            pltpu.VMEM(block, F32),
            pltpu.VMEM((4, GRP, TOK), F32),
            pltpu.VMEM((DP, 4, GRP, TOK), F32),
            pltpu.VMEM((2, CTX, 2 * GRP, TOK), BF16),
            pltpu.VMEM((2, CTX, 2 * GRP, TOK), BF16),
            pltpu.VMEM((DP, 4, GRP, TOK), F32),
            pltpu.VMEM((DP, 4, GRP, TOK), F32),
            pltpu.VMEM((4, GRP, TOK), F32),
            pltpu.VMEM((4, GRP, TOK), F32),
            pltpu.VMEM((DP, 4, GRP, TOK), F32),
            pltpu.VMEM((4, 24, TOK), F32),
            pltpu.VMEM((TOK, TOK), F32),
            pltpu.VMEM((24, GRP, TOK), F32),
            pltpu.VMEM(block, F32),
            pltpu.VMEM(block, F32),
            pltpu.VMEM(block, F32),
            pltpu.VMEM(block, F32),
            pltpu.VMEM(block, F32),
            pltpu.VMEM(block, F32),
            pltpu.VMEM(block, F32),
            pltpu.VMEM((4, 8, 2, GRP, TOK), F32),
            pltpu.VMEM((CTX, GRP, 4 * TOK), BF16),
            pltpu.VMEM((CTX, GRP, 2 * TOK), F32),
            pltpu.VMEM((CTX, GRP, 2 * TOK), F32),
            pltpu.VMEM((CTX, GRP, 2 * TOK), F32),
            pltpu.VMEM((CTX, GRP, 2 * TOK), F32),
            pltpu.VMEM((3, 24, TOK), F32),
            pltpu.VMEM((DP, 24, TOK), F32),
            pltpu.VMEM((8, 24, TOK), F32),
            pltpu.VMEM((4, 24, TOK), F32),
            pltpu.SemaphoreType.DMA((12,)),
            pltpu.SemaphoreType.DMA((12,)),
            pltpu.SemaphoreType.DMA((8,)),
        ],
        compiler_params=pltpu.CompilerParams(
            collective_id=0, has_side_effects=True, vmem_limit_bytes=40 << 20
        ),
        name="hyena",
    )(*operands)
    out, gfeat, gshort, gfilt, gskip = pl.pallas_call(
        deliver,
        out_shape=shapes,
        in_specs=[vmem] * 5,
        out_specs=(hbm,) * 5,
        scratch_shapes=[pltpu.SemaphoreType.DMA((5,))],
        compiler_params=pltpu.CompilerParams(vmem_limit_bytes=4 << 20),
        name="deliver",
    )(*results)
    return (out[None], gfeat[None], gshort, gfilt, gskip.reshape(CH))


def solution(mesh):
    return jax.shard_map(
        per_device,
        mesh=mesh,
        in_specs=(P("dp", "ctx", None), P(), P("ctx", None), P(), P("dp", "ctx", None)),
        out_specs=(P("dp", "ctx", None), P("dp", "ctx", None), P(), P("ctx", None), P()),
        check_vma=False,
    )
```

```python
import functools
import math

import jax
import jax.numpy as jnp
import ml_dtypes
import numpy as np
from jax import lax
from jax.experimental import pallas as pl
from jax.experimental.pallas import tpu as pltpu
from jax.sharding import PartitionSpec as P

MESH = pl.DeviceIdType.MESH
F32 = jnp.float32
BF16 = jnp.bfloat16

DP = 8
CTX = 32
TOK = 128
CH = 512
GRP = 16
TAPS = 7


def tables():
    index = np.arange(TOK)
    angle = 2.0 * np.pi * (np.outer(index, index) % TOK) / TOK
    cos, sin = np.cos(angle), np.sin(angle)
    forward = np.block([[cos, -sin], [sin, cos]])
    inverse = np.block([[cos, sin], [-sin, cos]]) / (CTX * TOK)
    parts = []
    for matrix in (forward, inverse):
        high = matrix.astype(np.float32).astype(ml_dtypes.bfloat16)
        low = (matrix - high.astype(np.float64)).astype(np.float32).astype(ml_dtypes.bfloat16)
        parts += [high, low]
    weights = np.stack(parts)
    inner = np.zeros((8, 8, TOK), np.float32)
    for a0 in range(8):
        for j0 in range(4):
            turn = -2.0 * np.pi * a0 * (1 + 4 * j0) / 128
            inner[a0, 2 * j0], inner[a0, 2 * j0 + 1] = np.cos(turn), np.sin(turn)
    outer = np.zeros((4, 16, TOK), np.float32)
    for j0 in range(4):
        for j1 in range(8):
            turn = -2.0 * np.pi * index * (4 * (j0 + 4 * j1) + 1) / 16384
            outer[j0, 2 * j1], outer[j0, 2 * j1 + 1] = np.cos(turn), np.sin(turn)
    return weights, inner, outer


COS1, SIN1 = math.cos(math.pi / 8), math.sin(math.pi / 8)
ROOT = math.sqrt(0.5)
COS3, SIN3 = math.cos(3 * math.pi / 8), math.sin(3 * math.pi / 8)


def cadd(x, y):
    return (x[0] + y[0], x[1] + y[1])


def csub(x, y):
    return (x[0] - y[0], x[1] - y[1])


def cmul(x, y):
    return (x[0] * y[0] - x[1] * y[1], x[0] * y[1] + x[1] * y[0])


def cmul_conj(x, y):
    return (x[0] * y[0] + x[1] * y[1], x[1] * y[0] - x[0] * y[1])


def turn(x, sign):
    return (-x[1], x[0]) if sign > 0 else (x[1], -x[0])


def dft4(x, sign):
    even, odd = cadd(x[0], x[2]), cadd(x[1], x[3])
    even1, odd1 = csub(x[0], x[2]), turn(csub(x[1], x[3]), sign)
    return [cadd(even, odd), cadd(even1, odd1), csub(even, odd), csub(even1, odd1)]


def dft8(x, sign):
    even = dft4(x[0::2], sign)
    odd = dft4(x[1::2], sign)
    first, third = odd[1], odd[3]
    if sign < 0:
        odd[1] = ((first[0] + first[1]) * ROOT, (first[1] - first[0]) * ROOT)
        odd[3] = ((third[1] - third[0]) * ROOT, (third[0] + third[1]) * -ROOT)
    else:
        odd[1] = ((first[0] - first[1]) * ROOT, (first[1] + first[0]) * ROOT)
        odd[3] = ((third[0] + third[1]) * -ROOT, (third[0] - third[1]) * ROOT)
    odd[2] = turn(odd[2], sign)
    return [cadd(even[k], odd[k]) for k in range(4)] + [csub(even[k], odd[k]) for k in range(4)]


def store_split(split_ref, slot, value):
    for half in range(2):
        high = value[half].astype(BF16)
        low = (value[half] - high.astype(F32)).astype(BF16)
        split_ref[slot, :, half * TOK : (half + 1) * TOK] = high
        split_ref[slot, :, (2 + half) * TOK : (3 + half) * TOK] = low


def product(split_ref, weights_ref, which, out_ref):
    dot = functools.partial(jnp.dot, preferred_element_type=F32)
    for start in range(0, CTX, 8):
        rows = slice(start, start + 8)
        high = split_ref[rows, :, : 2 * TOK].reshape(TOK, 2 * TOK)
        low = split_ref[rows, :, 2 * TOK :].reshape(TOK, 2 * TOK)
        total = dot(high, weights_ref[which + 1]) + dot(low, weights_ref[which])
        total = total + dot(high, weights_ref[which])
        out_ref[rows] = total.reshape(8, GRP, 2 * TOK)


def load_complex(ref, slot):
    return (ref[slot, :, :TOK], ref[slot, :, TOK:])


def transform(load, half_ref, split_ref, inner_ref, outer_ref, weights_ref, out_ref):
    def first(a0, carry):
        x0, x1, x2, x3 = [load(a0 + 8 * a1) for a1 in range(4)]
        t1 = (x1 * COS1, x1 * -SIN1)
        t2 = x2 * ROOT
        t3 = (x3 * COS3, x3 * -SIN3)
        even, even1 = (x0 + t2, -t2), (x0 - t2, t2)
        odd, odd1 = cadd(t1, t3), turn(csub(t1, t3), -1)
        for j0, value in enumerate([cadd(even, odd), cadd(even1, odd1), csub(even, odd), csub(even1, odd1)]):
            factor = (inner_ref[a0, 2 * j0 : 2 * j0 + 1, :], inner_ref[a0, 2 * j0 + 1 : 2 * j0 + 2, :])
            value = cmul(value, factor)
            half_ref[j0, a0, 0] = value[0]
            half_ref[j0, a0, 1] = value[1]
        return carry

    lax.fori_loop(0, 8, first, 0, unroll=2)

    def second(j0, carry):
        values = dft8([(half_ref[j0, a0, 0], half_ref[j0, a0, 1]) for a0 in range(8)], -1)
        for j1, value in enumerate(values):
            factor = (outer_ref[j0, 2 * j1 : 2 * j1 + 1, :], outer_ref[j0, 2 * j1 + 1 : 2 * j1 + 2, :])
            store_split(split_ref, j0 * 8 + j1, cmul(value, factor))
        return carry

    lax.fori_loop(0, 4, second, 0)
    product(split_ref, weights_ref, 0, out_ref)


def inverse(pair, emit, half_ref, split_ref, inner_ref, outer_ref, weights_ref, work_ref):
    def multiply(slot, carry):
        store_split(split_ref, slot, pair(slot))
        return carry

    lax.fori_loop(0, CTX, multiply, 0, unroll=4)
    product(split_ref, weights_ref, 2, work_ref)

    def second(j0, carry):
        values = []
        for j1 in range(8):
            factor = (outer_ref[j0, 2 * j1 : 2 * j1 + 1, :], outer_ref[j0, 2 * j1 + 1 : 2 * j1 + 2, :])
            values.append(cmul_conj(load_complex(work_ref, j0 * 8 + j1), factor))
        for a0, value in enumerate(dft8(values, 1)):
            half_ref[j0, a0, 0] = value[0]
            half_ref[j0, a0, 1] = value[1]
        return carry

    lax.fori_loop(0, 4, second, 0)

    def first(a0, carry):
        values = []
        for j0 in range(4):
            factor = (inner_ref[a0, 2 * j0 : 2 * j0 + 1, :], inner_ref[a0, 2 * j0 + 1 : 2 * j0 + 2, :])
            values.append(cmul_conj((half_ref[j0, a0, 0], half_ref[j0, a0, 1]), factor))
        z0, z1, z2, z3 = dft4(values, 1)
        emit(a0, z0[0])
        emit(a0 + 8, z1[0] * COS1 - z1[1] * SIN1)
        emit(a0 + 16, (z2[0] - z2[1]) * ROOT)
        emit(a0 + 24, z3[0] * COS3 - z3[1] * SIN3)
        return carry

    lax.fori_loop(0, 8, first, 0, unroll=2)


def kernel(
    feat_hbm, cot_hbm, filt_hbm, short_hbm, skip_hbm, weights_hbm, inner_hbm, outer_hbm,
    out_ref, gfeat_ref, gshort_ref, gfilt_ref, gskip_ref,
    feat_ref, cot_ref, filt_ref, short_ref, skip_ref, weights_ref, inner_ref, outer_ref,
    send_in, recv_in, send_filt, part_filt, all_filt, send_out, recv_out, send_corr, recv_corr,
    mine_corr, part_grad, all_grad, tap_rows, tap_cols, taps, key_ref, value_ref, query_ref,
    gated_ref, dconv_ref, conv_ref, dgated_ref, half_ref, split_ref, spec_g, spec_h, spec_d, work_ref,
    small_send, small_dp, small_ctx, sems_send, sems_recv, sems_load,
):
    loads = [
        pltpu.make_async_copy(source, target, sems_load.at[index])
        for index, (source, target) in enumerate(
            [
                (filt_hbm, filt_ref), (feat_hbm, feat_ref), (cot_hbm, cot_ref), (short_hbm, short_ref),
                (skip_hbm, skip_ref), (inner_hbm, inner_ref), (outer_hbm, outer_ref), (weights_hbm, weights_ref),
            ]
        )
    ]
    for load in loads:
        load.start()
    dp, me = lax.axis_index("dp"), lax.axis_index("ctx")
    zed, row = lax.rem(me, 8), me // 8
    owner = zed == dp
    owner_count = jnp.where(owner, 1, 0)
    lane = lax.broadcasted_iota(jnp.int32, (GRP, TOK), 1)
    scale = 1.0 / math.sqrt(DP * CTX * TOK)

    barrier = pltpu.get_barrier_semaphore()

    def greet(dp_index, ctx_index):
        pl.semaphore_signal(barrier, inc=1, device_id={"dp": dp_index, "ctx": ctx_index}, device_id_type=MESH)

    def greet_ctx(step, carry):
        greet(dp, lax.rem(me + step, CTX))
        return carry

    lax.fori_loop(1, CTX, greet_ctx, 0)

    def greet_dp(step, carry):
        greet(lax.rem(dp + step, DP), me)
        return carry

    lax.fori_loop(1, DP, greet_dp, 0)
    for x in range(4):

        @pl.when(jnp.logical_not(jnp.logical_and(owner, row == x)))
        def _():
            greet(zed, 8 * x + dp)

    def pack(block, part, slot, base):
        columns = [base + TOK * k for k in range(4)]
        for k, start in enumerate(columns):
            tile = block[:, start : start + TOK].T
            send_in[part, 8 * k : 8 * k + 8, slot * GRP : (slot + 1) * GRP, :] = tile.reshape(8, GRP, TOK)

    loads[0].wait()
    for k in range(4):
        send_filt[8 * k : 8 * k + 8] = filt_ref[:, k * TOK : (k + 1) * TOK].T.reshape(8, GRP, TOK)
    loads[1].wait()
    pack(feat_ref, 0, 0, CH)
    pack(feat_ref, 0, 1, 2 * CH)
    pack(feat_ref, 1, 0, 0)
    loads[2].wait()
    pack(cot_ref, 1, 1, 0)

    pl.semaphore_wait(barrier, (CTX - 1) + (DP - 1) + 4 - owner_count)

    def remote(src, dst, index, dp_index, ctx_index):
        return pltpu.make_async_remote_copy(
            src_ref=src,
            dst_ref=dst,
            send_sem=sems_send.at[index],
            recv_sem=sems_recv.at[index],
            device_id={"dp": dp_index, "ctx": ctx_index},
            device_id_type=MESH,
        )

    def await_bytes(ref, sem):
        pltpu.make_async_copy(ref, ref, sem).wait()

    def to_ctx(make):
        def step_to(step, carry):
            make(lax.rem(me + step, CTX)).start()
            return carry

        lax.fori_loop(1, CTX, step_to, 0)

    def to_dp(make):
        def step_to(step, carry):
            make(lax.rem(dp + step, DP)).start()
            return carry

        lax.fori_loop(1, DP, step_to, 0)

    def cross(source, target_ref, index):
        for x in range(4):
            itself = jnp.logical_and(owner, row == x)

            @pl.when(jnp.logical_not(itself))
            def _():
                remote(source(x), target_ref.at[row], index, zed, 8 * x + dp).start()

            @pl.when(itself)
            def _():
                pltpu.make_async_copy(source(x), target_ref.at[row], sems_recv.at[index]).start()

    cross(lambda x: send_filt.at[8 * x + dp], part_filt, 0)
    to_ctx(lambda c: remote(send_in.at[0, c], recv_in.at[0, me], 2, dp, c))
    to_ctx(lambda c: remote(send_in.at[1, c], recv_in.at[1, me], 3, dp, c))
    await_bytes(part_filt, sems_recv.at[0])
    to_dp(lambda d: remote(part_filt, all_filt.at[dp], 1, d, me))
    all_filt[dp] = part_filt[...]
    recv_in[0, me] = send_in[0, me]
    recv_in[1, me] = send_in[1, me]

    for load in loads[3:]:
        load.wait()

    for stream in range(3):
        for k in range(4):
            start = stream * CH + k * TOK
            tap_rows[k, 8 * stream : 8 * stream + TAPS, :] = short_ref[:, start : start + TOK]
            if stream == 0:
                tap_rows[k, TAPS : TAPS + 1, :] = skip_ref[:, k * TOK : (k + 1) * TOK]
            else:
                tap_rows[k, 8 * stream + TAPS : 8 * stream + 8, :] = jnp.zeros((1, TOK), F32)
    chosen = tap_rows[me // 8]
    tap_cols[...] = jnp.concatenate([chosen, jnp.zeros((TOK - 24, TOK), F32)], axis=0).T
    mine = tap_cols[pl.ds(pl.multiple_of(lax.rem(me, 8) * GRP, GRP), GRP), :]
    for index in range(24):
        taps[index] = jnp.broadcast_to(mine[:, index : index + 1], (GRP, TOK))

    common = (half_ref, split_ref, inner_ref, outer_ref, weights_ref)

    await_bytes(all_filt.at[pl.ds(0, DP - 1)], sems_recv.at[1])
    transform(lambda a: all_filt[lax.rem(a, 8), a // 8], *common, spec_h)

    def mix(source, before, first_tap):
        total = taps[first_tap] * source
        for tap in range(1, TAPS):
            moved = pltpu.roll(jnp.where(lane >= TOK - tap, before, source), tap, axis=1)
            total = total + taps[first_tap + tap] * moved
        return total

    await_bytes(recv_in.at[0, pl.ds(0, CTX - 1)], sems_recv.at[2])

    def mix_pair(a, carry):
        key = recv_in[0, a, :GRP, :].astype(F32)
        value = recv_in[0, a, GRP:, :].astype(F32)
        mixed_key = mix(key, carry[0], 8)
        mixed_value = mix(value, carry[1], 16)
        key_ref[a] = mixed_key
        value_ref[a] = mixed_value
        gated_ref[a] = mixed_key * mixed_value
        return (key, value)

    zero = jnp.zeros((GRP, TOK), F32)
    lax.fori_loop(0, CTX, mix_pair, (zero, zero), unroll=4)
    transform(lambda a: gated_ref[a], *common, spec_g)

    def emit_conv(a, value):
        conv_ref[a] = value + taps[TAPS] * gated_ref[a]

    inverse(lambda s: cmul(load_complex(spec_g, s), load_complex(spec_h, s)), emit_conv, *common, work_ref)

    await_bytes(recv_in.at[1, pl.ds(0, CTX - 1)], sems_recv.at[3])

    def mix_query(a, carry):
        query = recv_in[1, a, :GRP, :].astype(F32)
        mixed = mix(query, carry, 0)
        query_ref[a] = mixed
        dconv_ref[a] = mixed * recv_in[1, a, GRP:, :].astype(F32)
        return query

    lax.fori_loop(0, CTX, mix_query, zero, unroll=4)

    transform(lambda a: dconv_ref[a], *common, spec_d)

    def emit_corr(a, value):
        send_corr[lax.rem(a, 8), a // 8] = value * scale

    inverse(lambda s: cmul_conj(load_complex(spec_d, s), load_complex(spec_g, s)), emit_corr, *common, work_ref)
    to_dp(lambda d: remote(send_corr.at[d], recv_corr.at[dp], 6, d, me))
    recv_corr[dp] = send_corr[dp]

    def back_mix(current, after, first_tap, source, sums):
        total = taps[first_tap] * current
        out_sums = [sums[0] + current * source]
        for tap in range(1, TAPS):
            moved = pltpu.roll(jnp.where(lane < tap, after, current), TOK - tap, axis=1)
            total = total + taps[first_tap + tap] * moved
            out_sums.append(sums[tap] + moved * source)
        return total, out_sums

    def back_query(step, carry):
        a = CTX - 1 - step
        after, skip_sum, sums = carry[0], carry[1], carry[2:]
        conv = conv_ref[a]
        send_out[0, a, :GRP, :] = (query_ref[a] * conv).astype(BF16)
        current = recv_in[1, a, GRP:, :].astype(F32) * conv
        total, sums = back_mix(current, after, 0, recv_in[1, a, :GRP, :].astype(F32), sums)
        send_out[0, a, GRP:, :] = total.astype(BF16)
        return (current, skip_sum + dconv_ref[a] * gated_ref[a], *sums)

    sums_query = lax.fori_loop(0, CTX, back_query, (zero,) * 9, unroll=4)[1:]
    to_ctx(lambda c: remote(send_out.at[0, c], recv_out.at[0, me], 4, dp, c))
    recv_out[0, me] = send_out[0, me]

    def collect(start, columns, small):
        for offset, column in enumerate(columns):
            small = jnp.where(lane == start + offset, jnp.sum(column, axis=1, keepdims=True), small)
        return small

    small = collect(TAPS, sums_query[:1], zero)
    small = collect(0, sums_query[1:], small)

    def emit_back(a, value):
        dgated_ref[a] = value + taps[TAPS] * dconv_ref[a]

    inverse(lambda s: cmul_conj(load_complex(spec_d, s), load_complex(spec_h, s)), emit_back, *common, work_ref)

    for slot, (partner, first_tap) in enumerate([(value_ref, 8), (key_ref, 16)]):

        def back_pair(step, carry, slot=slot, partner=partner, first_tap=first_tap):
            a = CTX - 1 - step
            rows = slice(slot * GRP, (slot + 1) * GRP)
            current = dgated_ref[a] * partner[a]
            total, sums = back_mix(current, carry[0], first_tap, recv_in[0, a, rows, :].astype(F32), carry[1:])
            send_out[1, a, rows, :] = total.astype(BF16)
            return (current, *sums)

        small = collect(first_tap, lax.fori_loop(0, CTX, back_pair, (zero,) * 8, unroll=4)[1:], small)

    def summed(ref):
        total = ref[0]
        for index in range(1, 8):
            total = total + ref[index]
        return total

    await_bytes(recv_corr.at[pl.ds(0, DP - 1)], sems_recv.at[6])
    mine_corr[...] = summed(recv_corr)
    cross(lambda x: mine_corr.at[x], part_grad, 7)

    tap_cols[...] = jnp.zeros((TOK, TOK), F32)
    tap_cols[pl.ds(pl.multiple_of(zed * GRP, GRP), GRP), :] = small * scale
    turned = tap_cols[...].T
    tile = turned[:8, :]
    for stream in (1, 2):
        tile = tile + pltpu.roll(turned[8 * stream : 8 * stream + 8, :], GRP * stream, axis=1)
    small_send[0] = tile
    small_dp[dp] = tile
    to_dp(lambda d: remote(small_send.at[0], small_dp.at[dp], 8, d, me))
    to_ctx(lambda c: remote(send_out.at[1, c], recv_out.at[1, me], 5, dp, c))
    recv_out[1, me] = send_out[1, me]

    def unpack(part, slot, target_ref, base):
        for k in range(4):
            tile = recv_out[part, 8 * k : 8 * k + 8, slot * GRP : (slot + 1) * GRP, :].reshape(TOK, TOK)
            target_ref[:, base + k * TOK : base + (k + 1) * TOK] = tile.T

    await_bytes(small_dp.at[pl.ds(0, DP - 1)], sems_recv.at[8])
    small_send[1] = summed(small_dp)
    small_ctx[me] = small_send[1]
    to_ctx(lambda c: remote(small_send.at[1], small_ctx.at[me], 10, dp, c))

    await_bytes(part_grad, sems_recv.at[7])
    to_dp(lambda d: remote(part_grad, all_grad.at[dp], 9, d, me))
    all_grad[dp] = part_grad[...]

    await_bytes(recv_out.at[0, pl.ds(0, CTX - 1)], sems_recv.at[4])
    unpack(0, 0, out_ref, 0)
    unpack(0, 1, gfeat_ref, 0)
    await_bytes(recv_out.at[1, pl.ds(0, CTX - 1)], sems_recv.at[5])
    unpack(1, 0, gfeat_ref, CH)
    unpack(1, 1, gfeat_ref, 2 * CH)
    await_bytes(all_grad.at[pl.ds(0, DP - 1)], sems_recv.at[9])
    for x in range(4):
        gfilt_ref[:, x * TOK : (x + 1) * TOK] = all_grad[:, x].reshape(TOK, TOK).T

    await_bytes(small_ctx.at[pl.ds(0, CTX - 1)], sems_recv.at[10])
    place = lax.broadcasted_iota(jnp.int32, (8, TOK), 1) // GRP
    for x in range(4):
        for stream in range(3):
            rows = small_ctx[8 * x]
            for z in range(1, 8):
                rows = jnp.where(place == (z + stream) % 8, small_ctx[8 * x + z], rows)
            if stream:
                rows = pltpu.roll(rows, TOK - GRP * stream, axis=1)
            columns = slice(stream * CH + x * TOK, stream * CH + (x + 1) * TOK)
            gshort_ref[:, columns] = rows[:TAPS, :]
            if stream == 0:
                gskip_ref[:, columns] = rows[TAPS:, :]

    @pl.when(owner)
    def _():
        await_bytes(send_filt.at[pl.ds(0, 3)], sems_send.at[0])
        await_bytes(mine_corr.at[pl.ds(0, 3)], sems_send.at[7])

    @pl.when(jnp.logical_not(owner))
    def _():
        await_bytes(send_filt.at[pl.ds(0, 4)], sems_send.at[0])
        await_bytes(mine_corr.at[pl.ds(0, 4)], sems_send.at[7])

    await_bytes(all_filt.at[pl.ds(0, DP - 1)], sems_send.at[1])
    for part in range(2):
        await_bytes(send_in.at[part, pl.ds(0, CTX - 1)], sems_send.at[2 + part])
        await_bytes(send_out.at[part, pl.ds(0, CTX - 1)], sems_send.at[4 + part])
    await_bytes(send_corr.at[pl.ds(0, DP - 1)], sems_send.at[6])
    await_bytes(small_dp.at[pl.ds(0, DP - 1)], sems_send.at[8])
    await_bytes(all_grad.at[pl.ds(0, DP - 1)], sems_send.at[9])
    await_bytes(small_ctx.at[pl.ds(0, CTX - 1)], sems_send.at[10])


def deliver(*refs):
    sources, targets, sems = refs[:5], refs[5:10], refs[10]
    copies = [pltpu.make_async_copy(sources[index], targets[index], sems.at[index]) for index in range(5)]
    for copy in copies:
        copy.start()
    for copy in copies:
        copy.wait()


def per_device(features, short_weight, long_filter, skip_bias, cotangent):
    weights, inner, outer = tables()
    hbm = pl.BlockSpec(memory_space=pltpu.HBM)
    vmem = pl.BlockSpec(memory_space=pltpu.VMEM)
    block = (CTX, GRP, TOK)
    shapes = (
        jax.ShapeDtypeStruct((TOK, CH), BF16),
        jax.ShapeDtypeStruct((TOK, 3 * CH), BF16),
        jax.ShapeDtypeStruct((TAPS, 3 * CH), F32),
        jax.ShapeDtypeStruct((TOK, CH), F32),
        jax.ShapeDtypeStruct((1, CH), F32),
    )
    operands = [
        features[0], cotangent[0], long_filter, short_weight, skip_bias.reshape(1, CH),
        jnp.asarray(weights), jnp.asarray(inner), jnp.asarray(outer),
    ]
    operands = [pltpu.with_memory_space_constraint(operand, pltpu.HBM) for operand in operands]
    results = pl.pallas_call(
        kernel,
        out_shape=shapes,
        in_specs=[hbm] * 8,
        out_specs=(vmem,) * 5,
        scratch_shapes=[
            pltpu.VMEM((TOK, 3 * CH), BF16),
            pltpu.VMEM((TOK, CH), BF16),
            pltpu.VMEM((TOK, CH), F32),
            pltpu.VMEM((TAPS, 3 * CH), F32),
            pltpu.VMEM((1, CH), F32),
            pltpu.VMEM(weights.shape, BF16),
            pltpu.VMEM(inner.shape, F32),
            pltpu.VMEM(outer.shape, F32),
            pltpu.VMEM((2, CTX, 2 * GRP, TOK), BF16),
            pltpu.VMEM((2, CTX, 2 * GRP, TOK), BF16),
            pltpu.VMEM(block, F32),
            pltpu.VMEM((4, GRP, TOK), F32),
            pltpu.VMEM((DP, 4, GRP, TOK), F32),
            pltpu.VMEM((2, CTX, 2 * GRP, TOK), BF16),
            pltpu.VMEM((2, CTX, 2 * GRP, TOK), BF16),
            pltpu.VMEM((DP, 4, GRP, TOK), F32),
            pltpu.VMEM((DP, 4, GRP, TOK), F32),
            pltpu.VMEM((4, GRP, TOK), F32),
            pltpu.VMEM((4, GRP, TOK), F32),
            pltpu.VMEM((DP, 4, GRP, TOK), F32),
            pltpu.VMEM((4, 24, TOK), F32),
            pltpu.VMEM((TOK, TOK), F32),
            pltpu.VMEM((24, GRP, TOK), F32),
            pltpu.VMEM(block, F32),
            pltpu.VMEM(block, F32),
            pltpu.VMEM(block, F32),
            pltpu.VMEM(block, F32),
            pltpu.VMEM(block, F32),
            pltpu.VMEM(block, F32),
            pltpu.VMEM(block, F32),
            pltpu.VMEM((4, 8, 2, GRP, TOK), F32),
            pltpu.VMEM((CTX, GRP, 4 * TOK), BF16),
            pltpu.VMEM((CTX, GRP, 2 * TOK), F32),
            pltpu.VMEM((CTX, GRP, 2 * TOK), F32),
            pltpu.VMEM((CTX, GRP, 2 * TOK), F32),
            pltpu.VMEM((CTX, GRP, 2 * TOK), F32),
            pltpu.VMEM((2, 8, TOK), F32),
            pltpu.VMEM((DP, 8, TOK), F32),
            pltpu.VMEM((CTX, 8, TOK), F32),
            pltpu.SemaphoreType.DMA((12,)),
            pltpu.SemaphoreType.DMA((12,)),
            pltpu.SemaphoreType.DMA((8,)),
        ],
        compiler_params=pltpu.CompilerParams(
            collective_id=0, has_side_effects=True, vmem_limit_bytes=40 << 20
        ),
        name="hyena",
    )(*operands)
    out, gfeat, gshort, gfilt, gskip = pl.pallas_call(
        deliver,
        out_shape=shapes,
        in_specs=[vmem] * 5,
        out_specs=(hbm,) * 5,
        scratch_shapes=[pltpu.SemaphoreType.DMA((5,))],
        compiler_params=pltpu.CompilerParams(vmem_limit_bytes=4 << 20),
        name="deliver",
    )(*results)
    return (out[None], gfeat[None], gshort, gfilt, gskip.reshape(CH))


def solution(mesh):
    return jax.shard_map(
        per_device,
        mesh=mesh,
        in_specs=(P("dp", "ctx", None), P(), P("ctx", None), P(), P("dp", "ctx", None)),
        out_specs=(P("dp", "ctx", None), P("dp", "ctx", None), P(), P("ctx", None), P()),
        check_vma=False,
    )
```

```python
import functools
import math

import jax
import jax.numpy as jnp
import ml_dtypes
import numpy as np
from jax import lax
from jax.experimental import pallas as pl
from jax.experimental.pallas import tpu as pltpu
from jax.sharding import PartitionSpec as P

MESH = pl.DeviceIdType.MESH
F32 = jnp.float32
BF16 = jnp.bfloat16

DP = 8
CTX = 32
TOK = 128
CH = 512
GRP = 16
TAPS = 7


def tables():
    index = np.arange(TOK)
    angle = 2.0 * np.pi * (np.outer(index, index) % TOK) / TOK
    cos, sin = np.cos(angle), np.sin(angle)
    forward = np.block([[cos, -sin], [sin, cos]])
    inverse = np.block([[cos, sin], [-sin, cos]]) / (CTX * TOK)
    parts = []
    for matrix in (forward, inverse):
        high = matrix.astype(np.float32).astype(ml_dtypes.bfloat16)
        low = (matrix - high.astype(np.float64)).astype(np.float32).astype(ml_dtypes.bfloat16)
        parts += [high, low]
    weights = np.stack(parts)
    inner = np.zeros((8, 8, TOK), np.float32)
    for a0 in range(8):
        for j0 in range(4):
            turn = -2.0 * np.pi * a0 * (1 + 4 * j0) / 128
            inner[a0, 2 * j0], inner[a0, 2 * j0 + 1] = np.cos(turn), np.sin(turn)
    outer = np.zeros((4, 16, TOK), np.float32)
    for j0 in range(4):
        for j1 in range(8):
            turn = -2.0 * np.pi * index * (4 * (j0 + 4 * j1) + 1) / 16384
            outer[j0, 2 * j1], outer[j0, 2 * j1 + 1] = np.cos(turn), np.sin(turn)
    return weights, inner, outer


COS1, SIN1 = math.cos(math.pi / 8), math.sin(math.pi / 8)
ROOT = math.sqrt(0.5)
COS3, SIN3 = math.cos(3 * math.pi / 8), math.sin(3 * math.pi / 8)


def cadd(x, y):
    return (x[0] + y[0], x[1] + y[1])


def csub(x, y):
    return (x[0] - y[0], x[1] - y[1])


def cmul(x, y):
    return (x[0] * y[0] - x[1] * y[1], x[0] * y[1] + x[1] * y[0])


def cmul_conj(x, y):
    return (x[0] * y[0] + x[1] * y[1], x[1] * y[0] - x[0] * y[1])


def turn(x, sign):
    return (-x[1], x[0]) if sign > 0 else (x[1], -x[0])


def dft4(x, sign):
    even, odd = cadd(x[0], x[2]), cadd(x[1], x[3])
    even1, odd1 = csub(x[0], x[2]), turn(csub(x[1], x[3]), sign)
    return [cadd(even, odd), cadd(even1, odd1), csub(even, odd), csub(even1, odd1)]


def dft8(x, sign):
    even = dft4(x[0::2], sign)
    odd = dft4(x[1::2], sign)
    first, third = odd[1], odd[3]
    if sign < 0:
        odd[1] = ((first[0] + first[1]) * ROOT, (first[1] - first[0]) * ROOT)
        odd[3] = ((third[1] - third[0]) * ROOT, (third[0] + third[1]) * -ROOT)
    else:
        odd[1] = ((first[0] - first[1]) * ROOT, (first[1] + first[0]) * ROOT)
        odd[3] = ((third[0] + third[1]) * -ROOT, (third[0] - third[1]) * ROOT)
    odd[2] = turn(odd[2], sign)
    return [cadd(even[k], odd[k]) for k in range(4)] + [csub(even[k], odd[k]) for k in range(4)]


def store_split(split_ref, slot, value):
    for half in range(2):
        high = value[half].astype(BF16)
        low = (value[half] - high.astype(F32)).astype(BF16)
        split_ref[slot, :, half * TOK : (half + 1) * TOK] = high
        split_ref[slot, :, (2 + half) * TOK : (3 + half) * TOK] = low


def product(split_ref, weights_ref, which, out_ref):
    dot = functools.partial(jnp.dot, preferred_element_type=F32)
    for start in range(0, CTX, 8):
        rows = slice(start, start + 8)
        high = split_ref[rows, :, : 2 * TOK].reshape(TOK, 2 * TOK)
        low = split_ref[rows, :, 2 * TOK :].reshape(TOK, 2 * TOK)
        total = dot(high, weights_ref[which + 1]) + dot(low, weights_ref[which])
        total = total + dot(high, weights_ref[which])
        out_ref[rows] = total.reshape(8, GRP, 2 * TOK)


def load_complex(ref, slot):
    return (ref[slot, :, :TOK], ref[slot, :, TOK:])


def transform(load, half_ref, split_ref, inner_ref, outer_ref, weights_ref, out_ref):
    def first(a0, carry):
        x0, x1, x2, x3 = [load(a0 + 8 * a1) for a1 in range(4)]
        t1 = (x1 * COS1, x1 * -SIN1)
        t2 = x2 * ROOT
        t3 = (x3 * COS3, x3 * -SIN3)
        even, even1 = (x0 + t2, -t2), (x0 - t2, t2)
        odd, odd1 = cadd(t1, t3), turn(csub(t1, t3), -1)
        for j0, value in enumerate([cadd(even, odd), cadd(even1, odd1), csub(even, odd), csub(even1, odd1)]):
            factor = (inner_ref[a0, 2 * j0 : 2 * j0 + 1, :], inner_ref[a0, 2 * j0 + 1 : 2 * j0 + 2, :])
            value = cmul(value, factor)
            half_ref[j0, a0, 0] = value[0]
            half_ref[j0, a0, 1] = value[1]
        return carry

    lax.fori_loop(0, 8, first, 0, unroll=2)

    def second(j0, carry):
        values = dft8([(half_ref[j0, a0, 0], half_ref[j0, a0, 1]) for a0 in range(8)], -1)
        for j1, value in enumerate(values):
            factor = (outer_ref[j0, 2 * j1 : 2 * j1 + 1, :], outer_ref[j0, 2 * j1 + 1 : 2 * j1 + 2, :])
            store_split(split_ref, j0 * 8 + j1, cmul(value, factor))
        return carry

    lax.fori_loop(0, 4, second, 0)
    product(split_ref, weights_ref, 0, out_ref)


def inverse(pair, emit, half_ref, split_ref, inner_ref, outer_ref, weights_ref, work_ref):
    def multiply(slot, carry):
        store_split(split_ref, slot, pair(slot))
        return carry

    lax.fori_loop(0, CTX, multiply, 0, unroll=4)
    product(split_ref, weights_ref, 2, work_ref)

    def second(j0, carry):
        values = []
        for j1 in range(8):
            factor = (outer_ref[j0, 2 * j1 : 2 * j1 + 1, :], outer_ref[j0, 2 * j1 + 1 : 2 * j1 + 2, :])
            values.append(cmul_conj(load_complex(work_ref, j0 * 8 + j1), factor))
        for a0, value in enumerate(dft8(values, 1)):
            half_ref[j0, a0, 0] = value[0]
            half_ref[j0, a0, 1] = value[1]
        return carry

    lax.fori_loop(0, 4, second, 0)

    def first(a0, carry):
        values = []
        for j0 in range(4):
            factor = (inner_ref[a0, 2 * j0 : 2 * j0 + 1, :], inner_ref[a0, 2 * j0 + 1 : 2 * j0 + 2, :])
            values.append(cmul_conj((half_ref[j0, a0, 0], half_ref[j0, a0, 1]), factor))
        z0, z1, z2, z3 = dft4(values, 1)
        emit(a0, z0[0])
        emit(a0 + 8, z1[0] * COS1 - z1[1] * SIN1)
        emit(a0 + 16, (z2[0] - z2[1]) * ROOT)
        emit(a0 + 24, z3[0] * COS3 - z3[1] * SIN3)
        return carry

    lax.fori_loop(0, 8, first, 0, unroll=2)


def kernel(
    feat_hbm, cot_hbm, filt_hbm, short_hbm, skip_hbm, weights_hbm, inner_hbm, outer_hbm,
    out_ref, gfeat_ref, gshort_ref, gfilt_ref, gskip_ref,
    feat_ref, cot_ref, filt_ref, short_ref, skip_ref, weights_ref, inner_ref, outer_ref,
    send_in, recv_in, send_filt, part_filt, all_filt, send_out, recv_out, send_corr, recv_corr,
    mine_corr, part_grad, all_grad, tap_rows, tap_cols, taps, key_ref, value_ref, query_ref,
    gated_ref, dconv_ref, conv_ref, dgated_ref, half_ref, split_ref, spec_g, spec_h, spec_d, work_ref,
    small_send, small_dp, small_ctx, sems_send, sems_recv, sems_load,
):
    dp, me = lax.axis_index("dp"), lax.axis_index("ctx")
    zed, row = lax.rem(me, 8), me // 8
    owner = zed == dp
    owner_count = jnp.where(owner, 1, 0)
    lane = lax.broadcasted_iota(jnp.int32, (GRP, TOK), 1)
    scale = 1.0 / math.sqrt(DP * CTX * TOK)

    barrier = pltpu.get_barrier_semaphore()

    def greet(dp_index, ctx_index):
        pl.semaphore_signal(barrier, inc=1, device_id={"dp": dp_index, "ctx": ctx_index}, device_id_type=MESH)

    def greet_ctx(step, carry):
        greet(dp, lax.rem(me + step, CTX))
        return carry

    lax.fori_loop(1, CTX, greet_ctx, 0)

    def greet_dp(step, carry):
        greet(lax.rem(dp + step, DP), me)
        return carry

    lax.fori_loop(1, DP, greet_dp, 0)
    for x in range(4):

        @pl.when(jnp.logical_not(jnp.logical_and(owner, row == x)))
        def _():
            greet(zed, 8 * x + dp)

    loads = [
        pltpu.make_async_copy(source, target, sems_load.at[index])
        for index, (source, target) in enumerate(
            [
                (filt_hbm, filt_ref), (feat_hbm, feat_ref), (cot_hbm, cot_ref), (short_hbm, short_ref),
                (skip_hbm, skip_ref), (inner_hbm, inner_ref), (outer_hbm, outer_ref), (weights_hbm, weights_ref),
            ]
        )
    ]
    for load in loads:
        load.start()
    def pack(block, part, slot, base):
        columns = [base + TOK * k for k in range(4)]
        for k, start in enumerate(columns):
            tile = block[:, start : start + TOK].T
            send_in[part, 8 * k : 8 * k + 8, slot * GRP : (slot + 1) * GRP, :] = tile.reshape(8, GRP, TOK)

    loads[0].wait()
    for k in range(4):
        send_filt[8 * k : 8 * k + 8] = filt_ref[:, k * TOK : (k + 1) * TOK].T.reshape(8, GRP, TOK)
    loads[1].wait()
    pack(feat_ref, 0, 0, CH)
    pack(feat_ref, 0, 1, 2 * CH)
    pack(feat_ref, 1, 0, 0)
    loads[2].wait()
    pack(cot_ref, 1, 1, 0)

    pl.semaphore_wait(barrier, (CTX - 1) + (DP - 1) + 4 - owner_count)

    def remote(src, dst, index, dp_index, ctx_index):
        return pltpu.make_async_remote_copy(
            src_ref=src,
            dst_ref=dst,
            send_sem=sems_send.at[index],
            recv_sem=sems_recv.at[index],
            device_id={"dp": dp_index, "ctx": ctx_index},
            device_id_type=MESH,
        )

    def await_bytes(ref, sem):
        pltpu.make_async_copy(ref, ref, sem).wait()

    def to_ctx(make):
        def step_to(step, carry):
            make(lax.rem(me + step, CTX)).start()
            return carry

        lax.fori_loop(1, CTX, step_to, 0)

    def to_dp(make):
        def step_to(step, carry):
            make(lax.rem(dp + step, DP)).start()
            return carry

        lax.fori_loop(1, DP, step_to, 0)

    def cross(source, target_ref, index):
        for x in range(4):
            itself = jnp.logical_and(owner, row == x)

            @pl.when(jnp.logical_not(itself))
            def _():
                remote(source(x), target_ref.at[row], index, zed, 8 * x + dp).start()

            @pl.when(itself)
            def _():
                pltpu.make_async_copy(source(x), target_ref.at[row], sems_recv.at[index]).start()

    cross(lambda x: send_filt.at[8 * x + dp], part_filt, 0)
    to_ctx(lambda c: remote(send_in.at[0, c], recv_in.at[0, me], 2, dp, c))
    to_ctx(lambda c: remote(send_in.at[1, c], recv_in.at[1, me], 3, dp, c))
    await_bytes(part_filt, sems_recv.at[0])
    to_dp(lambda d: remote(part_filt, all_filt.at[dp], 1, d, me))
    all_filt[dp] = part_filt[...]
    recv_in[0, me] = send_in[0, me]
    recv_in[1, me] = send_in[1, me]

    for load in loads[3:]:
        load.wait()

    for stream in range(3):
        for k in range(4):
            start = stream * CH + k * TOK
            tap_rows[k, 8 * stream : 8 * stream + TAPS, :] = short_ref[:, start : start + TOK]
            if stream == 0:
                tap_rows[k, TAPS : TAPS + 1, :] = skip_ref[:, k * TOK : (k + 1) * TOK]
            else:
                tap_rows[k, 8 * stream + TAPS : 8 * stream + 8, :] = jnp.zeros((1, TOK), F32)
    chosen = tap_rows[me // 8]
    tap_cols[...] = jnp.concatenate([chosen, jnp.zeros((TOK - 24, TOK), F32)], axis=0).T
    mine = tap_cols[pl.ds(pl.multiple_of(lax.rem(me, 8) * GRP, GRP), GRP), :]
    for index in range(24):
        taps[index] = jnp.broadcast_to(mine[:, index : index + 1], (GRP, TOK))

    common = (half_ref, split_ref, inner_ref, outer_ref, weights_ref)

    await_bytes(all_filt.at[pl.ds(0, DP - 1)], sems_recv.at[1])
    transform(lambda a: all_filt[lax.rem(a, 8), a // 8], *common, spec_h)

    def mix(source, before, first_tap):
        total = taps[first_tap] * source
        for tap in range(1, TAPS):
            moved = pltpu.roll(jnp.where(lane >= TOK - tap, before, source), tap, axis=1)
            total = total + taps[first_tap + tap] * moved
        return total

    await_bytes(recv_in.at[0, pl.ds(0, CTX - 1)], sems_recv.at[2])

    def mix_pair(a, carry):
        key = recv_in[0, a, :GRP, :].astype(F32)
        value = recv_in[0, a, GRP:, :].astype(F32)
        mixed_key = mix(key, carry[0], 8)
        mixed_value = mix(value, carry[1], 16)
        key_ref[a] = mixed_key
        value_ref[a] = mixed_value
        gated_ref[a] = mixed_key * mixed_value
        return (key, value)

    zero = jnp.zeros((GRP, TOK), F32)
    lax.fori_loop(0, CTX, mix_pair, (zero, zero), unroll=4)
    transform(lambda a: gated_ref[a], *common, spec_g)

    def emit_conv(a, value):
        conv_ref[a] = value + taps[TAPS] * gated_ref[a]

    inverse(lambda s: cmul(load_complex(spec_g, s), load_complex(spec_h, s)), emit_conv, *common, work_ref)

    await_bytes(recv_in.at[1, pl.ds(0, CTX - 1)], sems_recv.at[3])

    def mix_query(a, carry):
        query = recv_in[1, a, :GRP, :].astype(F32)
        mixed = mix(query, carry, 0)
        query_ref[a] = mixed
        dconv_ref[a] = mixed * recv_in[1, a, GRP:, :].astype(F32)
        return query

    lax.fori_loop(0, CTX, mix_query, zero, unroll=8)

    transform(lambda a: dconv_ref[a], *common, spec_d)

    def emit_corr(a, value):
        send_corr[lax.rem(a, 8), a // 8] = value * scale

    inverse(lambda s: cmul_conj(load_complex(spec_d, s), load_complex(spec_g, s)), emit_corr, *common, work_ref)
    to_dp(lambda d: remote(send_corr.at[d], recv_corr.at[dp], 6, d, me))
    recv_corr[dp] = send_corr[dp]

    def back_mix(current, after, first_tap, source, sums):
        total = taps[first_tap] * current
        out_sums = [sums[0] + current * source]
        for tap in range(1, TAPS):
            moved = pltpu.roll(jnp.where(lane < tap, after, current), TOK - tap, axis=1)
            total = total + taps[first_tap + tap] * moved
            out_sums.append(sums[tap] + moved * source)
        return total, out_sums

    def back_query(step, carry):
        a = CTX - 1 - step
        after, skip_sum, sums = carry[0], carry[1], carry[2:]
        conv = conv_ref[a]
        send_out[0, a, :GRP, :] = (query_ref[a] * conv).astype(BF16)
        current = recv_in[1, a, GRP:, :].astype(F32) * conv
        total, sums = back_mix(current, after, 0, recv_in[1, a, :GRP, :].astype(F32), sums)
        send_out[0, a, GRP:, :] = total.astype(BF16)
        return (current, skip_sum + dconv_ref[a] * gated_ref[a], *sums)

    sums_query = lax.fori_loop(0, CTX, back_query, (zero,) * 9, unroll=8)[1:]
    to_ctx(lambda c: remote(send_out.at[0, c], recv_out.at[0, me], 4, dp, c))
    recv_out[0, me] = send_out[0, me]

    def collect(start, columns, small):
        for offset, column in enumerate(columns):
            small = jnp.where(lane == start + offset, jnp.sum(column, axis=1, keepdims=True), small)
        return small

    small = collect(TAPS, sums_query[:1], zero)
    small = collect(0, sums_query[1:], small)

    def emit_back(a, value):
        dgated_ref[a] = value + taps[TAPS] * dconv_ref[a]

    inverse(lambda s: cmul_conj(load_complex(spec_d, s), load_complex(spec_h, s)), emit_back, *common, work_ref)

    sums_pair = []
    for slot, (partner, first_tap) in enumerate([(value_ref, 8), (key_ref, 16)]):

        def back_pair(step, carry, slot=slot, partner=partner, first_tap=first_tap):
            a = CTX - 1 - step
            rows = slice(slot * GRP, (slot + 1) * GRP)
            current = dgated_ref[a] * partner[a]
            total, sums = back_mix(current, carry[0], first_tap, recv_in[0, a, rows, :].astype(F32), carry[1:])
            send_out[1, a, rows, :] = total.astype(BF16)
            return (current, *sums)

        sums_pair.append(lax.fori_loop(0, CTX, back_pair, (zero,) * 8, unroll=8)[1:])

    def summed(ref):
        total = ref[0]
        for index in range(1, 8):
            total = total + ref[index]
        return total

    await_bytes(recv_corr.at[pl.ds(0, DP - 1)], sems_recv.at[6])
    mine_corr[...] = summed(recv_corr)
    cross(lambda x: mine_corr.at[x], part_grad, 7)

    to_ctx(lambda c: remote(send_out.at[1, c], recv_out.at[1, me], 5, dp, c))

    for first_tap, sums in zip((8, 16), sums_pair):
        small = collect(first_tap, sums, small)
    tap_cols[...] = jnp.zeros((TOK, TOK), F32)
    tap_cols[pl.ds(pl.multiple_of(zed * GRP, GRP), GRP), :] = small * scale
    turned = tap_cols[...].T
    tile = turned[:8, :]
    for stream in (1, 2):
        tile = tile + pltpu.roll(turned[8 * stream : 8 * stream + 8, :], GRP * stream, axis=1)
    small_send[0] = tile
    small_dp[dp] = tile
    to_dp(lambda d: remote(small_send.at[0], small_dp.at[dp], 8, d, me))
    recv_out[1, me] = send_out[1, me]

    def unpack(part, slot, target_ref, base):
        for k in range(4):
            tile = recv_out[part, 8 * k : 8 * k + 8, slot * GRP : (slot + 1) * GRP, :].reshape(TOK, TOK)
            target_ref[:, base + k * TOK : base + (k + 1) * TOK] = tile.T

    await_bytes(small_dp.at[pl.ds(0, DP - 1)], sems_recv.at[8])
    small_send[1] = summed(small_dp)
    small_ctx[me] = small_send[1]
    to_ctx(lambda c: remote(small_send.at[1], small_ctx.at[me], 10, dp, c))

    await_bytes(part_grad, sems_recv.at[7])
    to_dp(lambda d: remote(part_grad, all_grad.at[dp], 9, d, me))
    all_grad[dp] = part_grad[...]

    await_bytes(recv_out.at[0, pl.ds(0, CTX - 1)], sems_recv.at[4])
    unpack(0, 0, out_ref, 0)
    unpack(0, 1, gfeat_ref, 0)
    await_bytes(all_grad.at[pl.ds(0, DP - 1)], sems_recv.at[9])
    for x in range(4):
        gfilt_ref[:, x * TOK : (x + 1) * TOK] = all_grad[:, x].reshape(TOK, TOK).T
    await_bytes(recv_out.at[1, pl.ds(0, CTX - 1)], sems_recv.at[5])
    unpack(1, 0, gfeat_ref, CH)
    unpack(1, 1, gfeat_ref, 2 * CH)

    await_bytes(small_ctx.at[pl.ds(0, CTX - 1)], sems_recv.at[10])
    place = lax.broadcasted_iota(jnp.int32, (8, TOK), 1) // GRP
    for x in range(4):
        for stream in range(3):
            rows = small_ctx[8 * x]
            for z in range(1, 8):
                rows = jnp.where(place == (z + stream) % 8, small_ctx[8 * x + z], rows)
            if stream:
                rows = pltpu.roll(rows, TOK - GRP * stream, axis=1)
            columns = slice(stream * CH + x * TOK, stream * CH + (x + 1) * TOK)
            gshort_ref[:, columns] = rows[:TAPS, :]
            if stream == 0:
                gskip_ref[:, columns] = rows[TAPS:, :]

    @pl.when(owner)
    def _():
        await_bytes(send_filt.at[pl.ds(0, 3)], sems_send.at[0])
        await_bytes(mine_corr.at[pl.ds(0, 3)], sems_send.at[7])

    @pl.when(jnp.logical_not(owner))
    def _():
        await_bytes(send_filt.at[pl.ds(0, 4)], sems_send.at[0])
        await_bytes(mine_corr.at[pl.ds(0, 4)], sems_send.at[7])

    await_bytes(all_filt.at[pl.ds(0, DP - 1)], sems_send.at[1])
    for part in range(2):
        await_bytes(send_in.at[part, pl.ds(0, CTX - 1)], sems_send.at[2 + part])
        await_bytes(send_out.at[part, pl.ds(0, CTX - 1)], sems_send.at[4 + part])
    await_bytes(send_corr.at[pl.ds(0, DP - 1)], sems_send.at[6])
    await_bytes(small_dp.at[pl.ds(0, DP - 1)], sems_send.at[8])
    await_bytes(all_grad.at[pl.ds(0, DP - 1)], sems_send.at[9])
    await_bytes(small_ctx.at[pl.ds(0, CTX - 1)], sems_send.at[10])


def deliver(*refs):
    sources, targets, sems = refs[:5], refs[5:10], refs[10]
    copies = [pltpu.make_async_copy(sources[index], targets[index], sems.at[index]) for index in range(5)]
    for copy in copies:
        copy.start()
    for copy in copies:
        copy.wait()


def per_device(features, short_weight, long_filter, skip_bias, cotangent):
    weights, inner, outer = tables()
    hbm = pl.BlockSpec(memory_space=pltpu.HBM)
    vmem = pl.BlockSpec(memory_space=pltpu.VMEM)
    block = (CTX, GRP, TOK)
    shapes = (
        jax.ShapeDtypeStruct((TOK, CH), BF16),
        jax.ShapeDtypeStruct((TOK, 3 * CH), BF16),
        jax.ShapeDtypeStruct((TAPS, 3 * CH), F32),
        jax.ShapeDtypeStruct((TOK, CH), F32),
        jax.ShapeDtypeStruct((1, CH), F32),
    )
    operands = [
        features[0], cotangent[0], long_filter, short_weight, skip_bias.reshape(1, CH),
        jnp.asarray(weights), jnp.asarray(inner), jnp.asarray(outer),
    ]
    operands = [pltpu.with_memory_space_constraint(operand, pltpu.HBM) for operand in operands]
    results = pl.pallas_call(
        kernel,
        out_shape=shapes,
        in_specs=[hbm] * 8,
        out_specs=(vmem,) * 5,
        scratch_shapes=[
            pltpu.VMEM((TOK, 3 * CH), BF16),
            pltpu.VMEM((TOK, CH), BF16),
            pltpu.VMEM((TOK, CH), F32),
            pltpu.VMEM((TAPS, 3 * CH), F32),
            pltpu.VMEM((1, CH), F32),
            pltpu.VMEM(weights.shape, BF16),
            pltpu.VMEM(inner.shape, F32),
            pltpu.VMEM(outer.shape, F32),
            pltpu.VMEM((2, CTX, 2 * GRP, TOK), BF16),
            pltpu.VMEM((2, CTX, 2 * GRP, TOK), BF16),
            pltpu.VMEM(block, F32),
            pltpu.VMEM((4, GRP, TOK), F32),
            pltpu.VMEM((DP, 4, GRP, TOK), F32),
            pltpu.VMEM((2, CTX, 2 * GRP, TOK), BF16),
            pltpu.VMEM((2, CTX, 2 * GRP, TOK), BF16),
            pltpu.VMEM((DP, 4, GRP, TOK), F32),
            pltpu.VMEM((DP, 4, GRP, TOK), F32),
            pltpu.VMEM((4, GRP, TOK), F32),
            pltpu.VMEM((4, GRP, TOK), F32),
            pltpu.VMEM((DP, 4, GRP, TOK), F32),
            pltpu.VMEM((4, 24, TOK), F32),
            pltpu.VMEM((TOK, TOK), F32),
            pltpu.VMEM((24, GRP, TOK), F32),
            pltpu.VMEM(block, F32),
            pltpu.VMEM(block, F32),
            pltpu.VMEM(block, F32),
            pltpu.VMEM(block, F32),
            pltpu.VMEM(block, F32),
            pltpu.VMEM(block, F32),
            pltpu.VMEM(block, F32),
            pltpu.VMEM((4, 8, 2, GRP, TOK), F32),
            pltpu.VMEM((CTX, GRP, 4 * TOK), BF16),
            pltpu.VMEM((CTX, GRP, 2 * TOK), F32),
            pltpu.VMEM((CTX, GRP, 2 * TOK), F32),
            pltpu.VMEM((CTX, GRP, 2 * TOK), F32),
            pltpu.VMEM((CTX, GRP, 2 * TOK), F32),
            pltpu.VMEM((2, 8, TOK), F32),
            pltpu.VMEM((DP, 8, TOK), F32),
            pltpu.VMEM((CTX, 8, TOK), F32),
            pltpu.SemaphoreType.DMA((12,)),
            pltpu.SemaphoreType.DMA((12,)),
            pltpu.SemaphoreType.DMA((8,)),
        ],
        compiler_params=pltpu.CompilerParams(
            collective_id=0, has_side_effects=True, vmem_limit_bytes=40 << 20
        ),
        name="hyena",
    )(*operands)
    out, gfeat, gshort, gfilt, gskip = pl.pallas_call(
        deliver,
        out_shape=shapes,
        in_specs=[vmem] * 5,
        out_specs=(hbm,) * 5,
        scratch_shapes=[pltpu.SemaphoreType.DMA((5,))],
        compiler_params=pltpu.CompilerParams(vmem_limit_bytes=4 << 20),
        name="deliver",
    )(*results)
    return (out[None], gfeat[None], gshort, gfilt, gskip.reshape(CH))


def solution(mesh):
    return jax.shard_map(
        per_device,
        mesh=mesh,
        in_specs=(P("dp", "ctx", None), P(), P("ctx", None), P(), P("dp", "ctx", None)),
        out_specs=(P("dp", "ctx", None), P("dp", "ctx", None), P(), P("ctx", None), P()),
        check_vma=False,
    )
```

```python
import functools
import math

import jax
import jax.numpy as jnp
import ml_dtypes
import numpy as np
from jax import lax
from jax.experimental import pallas as pl
from jax.experimental.pallas import tpu as pltpu
from jax.sharding import PartitionSpec as P

MESH = pl.DeviceIdType.MESH
F32 = jnp.float32
BF16 = jnp.bfloat16

DP = 8
CTX = 32
TOK = 128
CH = 512
GRP = 16
TAPS = 7


def tables():
    index = np.arange(TOK)
    angle = 2.0 * np.pi * (np.outer(index, index) % TOK) / TOK
    cos, sin = np.cos(angle), np.sin(angle)
    forward = np.block([[cos, -sin], [sin, cos]])
    inverse = np.block([[cos, sin], [-sin, cos]]) / (CTX * TOK)
    parts = []
    for matrix in (forward, inverse):
        high = matrix.astype(np.float32).astype(ml_dtypes.bfloat16)
        low = (matrix - high.astype(np.float64)).astype(np.float32).astype(ml_dtypes.bfloat16)
        parts += [high, low]
    weights = np.stack(parts)
    inner = np.zeros((8, 8, TOK), np.float32)
    for a0 in range(8):
        for j0 in range(4):
            turn = -2.0 * np.pi * a0 * (1 + 4 * j0) / 128
            inner[a0, 2 * j0], inner[a0, 2 * j0 + 1] = np.cos(turn), np.sin(turn)
    outer = np.zeros((4, 16, TOK), np.float32)
    for j0 in range(4):
        for j1 in range(8):
            turn = -2.0 * np.pi * index * (4 * (j0 + 4 * j1) + 1) / 16384
            outer[j0, 2 * j1], outer[j0, 2 * j1 + 1] = np.cos(turn), np.sin(turn)
    return weights, inner, outer


COS1, SIN1 = math.cos(math.pi / 8), math.sin(math.pi / 8)
ROOT = math.sqrt(0.5)
COS3, SIN3 = math.cos(3 * math.pi / 8), math.sin(3 * math.pi / 8)


def cadd(x, y):
    return (x[0] + y[0], x[1] + y[1])


def csub(x, y):
    return (x[0] - y[0], x[1] - y[1])


def cmul(x, y):
    return (x[0] * y[0] - x[1] * y[1], x[0] * y[1] + x[1] * y[0])


def cmul_conj(x, y):
    return (x[0] * y[0] + x[1] * y[1], x[1] * y[0] - x[0] * y[1])


def turn(x, sign):
    return (-x[1], x[0]) if sign > 0 else (x[1], -x[0])


def dft4(x, sign):
    even, odd = cadd(x[0], x[2]), cadd(x[1], x[3])
    even1, odd1 = csub(x[0], x[2]), turn(csub(x[1], x[3]), sign)
    return [cadd(even, odd), cadd(even1, odd1), csub(even, odd), csub(even1, odd1)]


def dft8(x, sign):
    even = dft4(x[0::2], sign)
    odd = dft4(x[1::2], sign)
    first, third = odd[1], odd[3]
    if sign < 0:
        odd[1] = ((first[0] + first[1]) * ROOT, (first[1] - first[0]) * ROOT)
        odd[3] = ((third[1] - third[0]) * ROOT, (third[0] + third[1]) * -ROOT)
    else:
        odd[1] = ((first[0] - first[1]) * ROOT, (first[1] + first[0]) * ROOT)
        odd[3] = ((third[0] + third[1]) * -ROOT, (third[0] - third[1]) * ROOT)
    odd[2] = turn(odd[2], sign)
    return [cadd(even[k], odd[k]) for k in range(4)] + [csub(even[k], odd[k]) for k in range(4)]


def store_split(split_ref, slot, value):
    for half in range(2):
        high = value[half].astype(BF16)
        low = (value[half] - high.astype(F32)).astype(BF16)
        split_ref[slot, :, half * TOK : (half + 1) * TOK] = high
        split_ref[slot, :, (2 + half) * TOK : (3 + half) * TOK] = low


def product(split_ref, weights_ref, which, out_ref):
    dot = functools.partial(jnp.dot, preferred_element_type=F32)
    for start in range(0, CTX, 8):
        rows = slice(start, start + 8)
        high = split_ref[rows, :, : 2 * TOK].reshape(TOK, 2 * TOK)
        low = split_ref[rows, :, 2 * TOK :].reshape(TOK, 2 * TOK)
        total = dot(high, weights_ref[which + 1]) + dot(low, weights_ref[which])
        total = total + dot(high, weights_ref[which])
        out_ref[rows] = total.reshape(8, GRP, 2 * TOK)


def load_complex(ref, slot):
    return (ref[slot, :, :TOK], ref[slot, :, TOK:])


def transform(load, half_ref, split_ref, inner_ref, outer_ref, weights_ref, out_ref):
    def first(a0, carry):
        x0, x1, x2, x3 = [load(a0 + 8 * a1) for a1 in range(4)]
        t1 = (x1 * COS1, x1 * -SIN1)
        t2 = x2 * ROOT
        t3 = (x3 * COS3, x3 * -SIN3)
        even, even1 = (x0 + t2, -t2), (x0 - t2, t2)
        odd, odd1 = cadd(t1, t3), turn(csub(t1, t3), -1)
        for j0, value in enumerate([cadd(even, odd), cadd(even1, odd1), csub(even, odd), csub(even1, odd1)]):
            factor = (inner_ref[a0, 2 * j0 : 2 * j0 + 1, :], inner_ref[a0, 2 * j0 + 1 : 2 * j0 + 2, :])
            value = cmul(value, factor)
            half_ref[j0, a0, 0] = value[0]
            half_ref[j0, a0, 1] = value[1]
        return carry

    lax.fori_loop(0, 8, first, 0, unroll=4)

    def second(j0, carry):
        values = dft8([(half_ref[j0, a0, 0], half_ref[j0, a0, 1]) for a0 in range(8)], -1)
        for j1, value in enumerate(values):
            factor = (outer_ref[j0, 2 * j1 : 2 * j1 + 1, :], outer_ref[j0, 2 * j1 + 1 : 2 * j1 + 2, :])
            store_split(split_ref, j0 * 8 + j1, cmul(value, factor))
        return carry

    lax.fori_loop(0, 4, second, 0, unroll=2)
    product(split_ref, weights_ref, 0, out_ref)


def inverse(pair, emit, half_ref, split_ref, inner_ref, outer_ref, weights_ref, work_ref):
    def multiply(slot, carry):
        store_split(split_ref, slot, pair(slot))
        return carry

    lax.fori_loop(0, CTX, multiply, 0, unroll=8)
    product(split_ref, weights_ref, 2, work_ref)

    def second(j0, carry):
        values = []
        for j1 in range(8):
            factor = (outer_ref[j0, 2 * j1 : 2 * j1 + 1, :], outer_ref[j0, 2 * j1 + 1 : 2 * j1 + 2, :])
            values.append(cmul_conj(load_complex(work_ref, j0 * 8 + j1), factor))
        for a0, value in enumerate(dft8(values, 1)):
            half_ref[j0, a0, 0] = value[0]
            half_ref[j0, a0, 1] = value[1]
        return carry

    lax.fori_loop(0, 4, second, 0, unroll=2)

    def first(a0, carry):
        values = []
        for j0 in range(4):
            factor = (inner_ref[a0, 2 * j0 : 2 * j0 + 1, :], inner_ref[a0, 2 * j0 + 1 : 2 * j0 + 2, :])
            values.append(cmul_conj((half_ref[j0, a0, 0], half_ref[j0, a0, 1]), factor))
        z0, z1, z2, z3 = dft4(values, 1)
        emit(a0, z0[0])
        emit(a0 + 8, z1[0] * COS1 - z1[1] * SIN1)
        emit(a0 + 16, (z2[0] - z2[1]) * ROOT)
        emit(a0 + 24, z3[0] * COS3 - z3[1] * SIN3)
        return carry

    lax.fori_loop(0, 8, first, 0, unroll=4)


def kernel(
    feat_hbm, cot_hbm, filt_hbm, short_hbm, skip_hbm, weights_hbm, inner_hbm, outer_hbm,
    out_ref, gfeat_ref, gshort_ref, gfilt_ref, gskip_ref,
    feat_ref, cot_ref, filt_ref, short_ref, skip_ref, weights_ref, inner_ref, outer_ref,
    send_in, recv_in, send_filt, part_filt, all_filt, send_out, recv_out, send_corr, recv_corr,
    mine_corr, part_grad, all_grad, tap_rows, tap_cols, taps, key_ref, value_ref, query_ref,
    gated_ref, dconv_ref, conv_ref, dgated_ref, half_ref, split_ref, spec_g, spec_h, spec_d, work_ref,
    small_send, small_dp, small_ctx, sems_send, sems_recv, sems_load,
):
    dp, me = lax.axis_index("dp"), lax.axis_index("ctx")
    zed, row = lax.rem(me, 8), me // 8
    owner = zed == dp
    owner_count = jnp.where(owner, 1, 0)
    lane = lax.broadcasted_iota(jnp.int32, (GRP, TOK), 1)
    scale = 1.0 / math.sqrt(DP * CTX * TOK)

    barrier = pltpu.get_barrier_semaphore()

    def greet(dp_index, ctx_index):
        pl.semaphore_signal(barrier, inc=1, device_id={"dp": dp_index, "ctx": ctx_index}, device_id_type=MESH)

    def greet_ctx(step, carry):
        greet(dp, lax.rem(me + step, CTX))
        return carry

    lax.fori_loop(1, CTX, greet_ctx, 0)

    def greet_dp(step, carry):
        greet(lax.rem(dp + step, DP), me)
        return carry

    lax.fori_loop(1, DP, greet_dp, 0)
    for x in range(4):

        @pl.when(jnp.logical_not(jnp.logical_and(owner, row == x)))
        def _():
            greet(zed, 8 * x + dp)

    loads = [
        pltpu.make_async_copy(source, target, sems_load.at[index])
        for index, (source, target) in enumerate(
            [
                (filt_hbm, filt_ref), (feat_hbm, feat_ref), (cot_hbm, cot_ref), (short_hbm, short_ref),
                (skip_hbm, skip_ref), (inner_hbm, inner_ref), (outer_hbm, outer_ref), (weights_hbm, weights_ref),
            ]
        )
    ]
    for load in loads:
        load.start()
    def pack(block, part, slot, base):
        columns = [base + TOK * k for k in range(4)]
        for k, start in enumerate(columns):
            tile = block[:, start : start + TOK].T
            send_in[part, 8 * k : 8 * k + 8, slot * GRP : (slot + 1) * GRP, :] = tile.reshape(8, GRP, TOK)

    loads[0].wait()
    for k in range(4):
        send_filt[8 * k : 8 * k + 8] = filt_ref[:, k * TOK : (k + 1) * TOK].T.reshape(8, GRP, TOK)
    loads[1].wait()
    pack(feat_ref, 0, 0, CH)
    pack(feat_ref, 0, 1, 2 * CH)
    pack(feat_ref, 1, 0, 0)
    loads[2].wait()
    pack(cot_ref, 1, 1, 0)

    pl.semaphore_wait(barrier, (CTX - 1) + (DP - 1) + 4 - owner_count)

    def remote(src, dst, index, dp_index, ctx_index):
        return pltpu.make_async_remote_copy(
            src_ref=src,
            dst_ref=dst,
            send_sem=sems_send.at[index],
            recv_sem=sems_recv.at[index],
            device_id={"dp": dp_index, "ctx": ctx_index},
            device_id_type=MESH,
        )

    def await_bytes(ref, sem):
        pltpu.make_async_copy(ref, ref, sem).wait()

    def to_ctx(make):
        def step_to(step, carry):
            make(lax.rem(me + step, CTX)).start()
            return carry

        lax.fori_loop(1, CTX, step_to, 0)

    def to_dp(make):
        def step_to(step, carry):
            make(lax.rem(dp + step, DP)).start()
            return carry

        lax.fori_loop(1, DP, step_to, 0)

    def cross(source, target_ref, index):
        for x in range(4):
            itself = jnp.logical_and(owner, row == x)

            @pl.when(jnp.logical_not(itself))
            def _():
                remote(source(x), target_ref.at[row], index, zed, 8 * x + dp).start()

            @pl.when(itself)
            def _():
                pltpu.make_async_copy(source(x), target_ref.at[row], sems_recv.at[index]).start()

    cross(lambda x: send_filt.at[8 * x + dp], part_filt, 0)
    to_ctx(lambda c: remote(send_in.at[0, c], recv_in.at[0, me], 2, dp, c))
    to_ctx(lambda c: remote(send_in.at[1, c], recv_in.at[1, me], 3, dp, c))
    await_bytes(part_filt, sems_recv.at[0])
    to_dp(lambda d: remote(part_filt, all_filt.at[dp], 1, d, me))
    all_filt[dp] = part_filt[...]
    recv_in[0, me] = send_in[0, me]
    recv_in[1, me] = send_in[1, me]

    for load in loads[3:]:
        load.wait()

    for stream in range(3):
        for k in range(4):
            start = stream * CH + k * TOK
            tap_rows[k, 8 * stream : 8 * stream + TAPS, :] = short_ref[:, start : start + TOK]
            if stream == 0:
                tap_rows[k, TAPS : TAPS + 1, :] = skip_ref[:, k * TOK : (k + 1) * TOK]
            else:
                tap_rows[k, 8 * stream + TAPS : 8 * stream + 8, :] = jnp.zeros((1, TOK), F32)
    chosen = tap_rows[me // 8]
    tap_cols[...] = jnp.concatenate([chosen, jnp.zeros((TOK - 24, TOK), F32)], axis=0).T
    mine = tap_cols[pl.ds(pl.multiple_of(lax.rem(me, 8) * GRP, GRP), GRP), :]
    for index in range(24):
        taps[index] = jnp.broadcast_to(mine[:, index : index + 1], (GRP, TOK))

    common = (half_ref, split_ref, inner_ref, outer_ref, weights_ref)

    await_bytes(all_filt.at[pl.ds(0, DP - 1)], sems_recv.at[1])
    transform(lambda a: all_filt[lax.rem(a, 8), a // 8], *common, spec_h)

    def mix(source, before, first_tap):
        total = taps[first_tap] * source
        for tap in range(1, TAPS):
            moved = pltpu.roll(jnp.where(lane >= TOK - tap, before, source), tap, axis=1)
            total = total + taps[first_tap + tap] * moved
        return total

    await_bytes(recv_in.at[0, pl.ds(0, CTX - 1)], sems_recv.at[2])

    def mix_pair(a, carry):
        key = recv_in[0, a, :GRP, :].astype(F32)
        value = recv_in[0, a, GRP:, :].astype(F32)
        mixed_key = mix(key, carry[0], 8)
        mixed_value = mix(value, carry[1], 16)
        key_ref[a] = mixed_key
        value_ref[a] = mixed_value
        gated_ref[a] = mixed_key * mixed_value
        return (key, value)

    zero = jnp.zeros((GRP, TOK), F32)
    lax.fori_loop(0, CTX, mix_pair, (zero, zero), unroll=4)
    transform(lambda a: gated_ref[a], *common, spec_g)

    def emit_conv(a, value):
        conv_ref[a] = value + taps[TAPS] * gated_ref[a]

    inverse(lambda s: cmul(load_complex(spec_g, s), load_complex(spec_h, s)), emit_conv, *common, work_ref)

    await_bytes(recv_in.at[1, pl.ds(0, CTX - 1)], sems_recv.at[3])

    def mix_query(a, carry):
        query = recv_in[1, a, :GRP, :].astype(F32)
        mixed = mix(query, carry, 0)
        query_ref[a] = mixed
        dconv_ref[a] = mixed * recv_in[1, a, GRP:, :].astype(F32)
        return query

    lax.fori_loop(0, CTX, mix_query, zero, unroll=8)

    transform(lambda a: dconv_ref[a], *common, spec_d)

    def emit_corr(a, value):
        send_corr[lax.rem(a, 8), a // 8] = value * scale

    inverse(lambda s: cmul_conj(load_complex(spec_d, s), load_complex(spec_g, s)), emit_corr, *common, work_ref)
    to_dp(lambda d: remote(send_corr.at[d], recv_corr.at[dp], 6, d, me))
    recv_corr[dp] = send_corr[dp]

    def back_mix(current, after, first_tap, source, sums):
        total = taps[first_tap] * current
        out_sums = [sums[0] + current * source]
        for tap in range(1, TAPS):
            moved = pltpu.roll(jnp.where(lane < tap, after, current), TOK - tap, axis=1)
            total = total + taps[first_tap + tap] * moved
            out_sums.append(sums[tap] + moved * source)
        return total, out_sums

    def back_query(step, carry):
        a = CTX - 1 - step
        after, skip_sum, sums = carry[0], carry[1], carry[2:]
        conv = conv_ref[a]
        send_out[0, a, :GRP, :] = (query_ref[a] * conv).astype(BF16)
        current = recv_in[1, a, GRP:, :].astype(F32) * conv
        total, sums = back_mix(current, after, 0, recv_in[1, a, :GRP, :].astype(F32), sums)
        send_out[0, a, GRP:, :] = total.astype(BF16)
        return (current, skip_sum + dconv_ref[a] * gated_ref[a], *sums)

    sums_query = lax.fori_loop(0, CTX, back_query, (zero,) * 9, unroll=8)[1:]
    to_ctx(lambda c: remote(send_out.at[0, c], recv_out.at[0, me], 4, dp, c))
    recv_out[0, me] = send_out[0, me]

    def collect(start, columns, small):
        for offset, column in enumerate(columns):
            small = jnp.where(lane == start + offset, jnp.sum(column, axis=1, keepdims=True), small)
        return small

    small = collect(TAPS, sums_query[:1], zero)
    small = collect(0, sums_query[1:], small)

    def emit_back(a, value):
        dgated_ref[a] = value + taps[TAPS] * dconv_ref[a]

    inverse(lambda s: cmul_conj(load_complex(spec_d, s), load_complex(spec_h, s)), emit_back, *common, work_ref)

    sums_pair = []
    for slot, (partner, first_tap) in enumerate([(value_ref, 8), (key_ref, 16)]):

        def back_pair(step, carry, slot=slot, partner=partner, first_tap=first_tap):
            a = CTX - 1 - step
            rows = slice(slot * GRP, (slot + 1) * GRP)
            current = dgated_ref[a] * partner[a]
            total, sums = back_mix(current, carry[0], first_tap, recv_in[0, a, rows, :].astype(F32), carry[1:])
            send_out[1, a, rows, :] = total.astype(BF16)
            return (current, *sums)

        sums_pair.append(lax.fori_loop(0, CTX, back_pair, (zero,) * 8, unroll=8)[1:])

    def summed(ref):
        total = ref[0]
        for index in range(1, 8):
            total = total + ref[index]
        return total

    await_bytes(recv_corr.at[pl.ds(0, DP - 1)], sems_recv.at[6])
    mine_corr[...] = summed(recv_corr)
    cross(lambda x: mine_corr.at[x], part_grad, 7)

    to_ctx(lambda c: remote(send_out.at[1, c], recv_out.at[1, me], 5, dp, c))

    for first_tap, sums in zip((8, 16), sums_pair):
        small = collect(first_tap, sums, small)
    tap_cols[...] = jnp.zeros((TOK, TOK), F32)
    tap_cols[pl.ds(pl.multiple_of(zed * GRP, GRP), GRP), :] = small * scale
    turned = tap_cols[...].T
    tile = turned[:8, :]
    for stream in (1, 2):
        tile = tile + pltpu.roll(turned[8 * stream : 8 * stream + 8, :], GRP * stream, axis=1)
    small_send[0] = tile
    small_dp[dp] = tile
    to_dp(lambda d: remote(small_send.at[0], small_dp.at[dp], 8, d, me))
    recv_out[1, me] = send_out[1, me]

    def unpack(part, slot, target_ref, base):
        for k in range(4):
            tile = recv_out[part, 8 * k : 8 * k + 8, slot * GRP : (slot + 1) * GRP, :].reshape(TOK, TOK)
            target_ref[:, base + k * TOK : base + (k + 1) * TOK] = tile.T

    await_bytes(small_dp.at[pl.ds(0, DP - 1)], sems_recv.at[8])
    small_send[1] = summed(small_dp)
    small_ctx[me] = small_send[1]
    to_ctx(lambda c: remote(small_send.at[1], small_ctx.at[me], 10, dp, c))

    await_bytes(part_grad, sems_recv.at[7])
    to_dp(lambda d: remote(part_grad, all_grad.at[dp], 9, d, me))
    all_grad[dp] = part_grad[...]

    await_bytes(recv_out.at[0, pl.ds(0, CTX - 1)], sems_recv.at[4])
    unpack(0, 0, out_ref, 0)
    unpack(0, 1, gfeat_ref, 0)
    await_bytes(all_grad.at[pl.ds(0, DP - 1)], sems_recv.at[9])
    for x in range(4):
        gfilt_ref[:, x * TOK : (x + 1) * TOK] = all_grad[:, x].reshape(TOK, TOK).T
    await_bytes(recv_out.at[1, pl.ds(0, CTX - 1)], sems_recv.at[5])
    unpack(1, 0, gfeat_ref, CH)
    unpack(1, 1, gfeat_ref, 2 * CH)

    await_bytes(small_ctx.at[pl.ds(0, CTX - 1)], sems_recv.at[10])
    place = lax.broadcasted_iota(jnp.int32, (8, TOK), 1) // GRP
    for x in range(4):
        for stream in range(3):
            rows = small_ctx[8 * x]
            for z in range(1, 8):
                rows = jnp.where(place == (z + stream) % 8, small_ctx[8 * x + z], rows)
            if stream:
                rows = pltpu.roll(rows, TOK - GRP * stream, axis=1)
            columns = slice(stream * CH + x * TOK, stream * CH + (x + 1) * TOK)
            gshort_ref[:, columns] = rows[:TAPS, :]
            if stream == 0:
                gskip_ref[:, columns] = rows[TAPS:, :]

    @pl.when(owner)
    def _():
        await_bytes(send_filt.at[pl.ds(0, 3)], sems_send.at[0])
        await_bytes(mine_corr.at[pl.ds(0, 3)], sems_send.at[7])

    @pl.when(jnp.logical_not(owner))
    def _():
        await_bytes(send_filt.at[pl.ds(0, 4)], sems_send.at[0])
        await_bytes(mine_corr.at[pl.ds(0, 4)], sems_send.at[7])

    await_bytes(all_filt.at[pl.ds(0, DP - 1)], sems_send.at[1])
    for part in range(2):
        await_bytes(send_in.at[part, pl.ds(0, CTX - 1)], sems_send.at[2 + part])
        await_bytes(send_out.at[part, pl.ds(0, CTX - 1)], sems_send.at[4 + part])
    await_bytes(send_corr.at[pl.ds(0, DP - 1)], sems_send.at[6])
    await_bytes(small_dp.at[pl.ds(0, DP - 1)], sems_send.at[8])
    await_bytes(all_grad.at[pl.ds(0, DP - 1)], sems_send.at[9])
    await_bytes(small_ctx.at[pl.ds(0, CTX - 1)], sems_send.at[10])


def deliver(*refs):
    sources, targets, sems = refs[:5], refs[5:10], refs[10]
    copies = [pltpu.make_async_copy(sources[index], targets[index], sems.at[index]) for index in range(5)]
    for copy in copies:
        copy.start()
    for copy in copies:
        copy.wait()


def per_device(features, short_weight, long_filter, skip_bias, cotangent):
    weights, inner, outer = tables()
    hbm = pl.BlockSpec(memory_space=pltpu.HBM)
    vmem = pl.BlockSpec(memory_space=pltpu.VMEM)
    block = (CTX, GRP, TOK)
    shapes = (
        jax.ShapeDtypeStruct((TOK, CH), BF16),
        jax.ShapeDtypeStruct((TOK, 3 * CH), BF16),
        jax.ShapeDtypeStruct((TAPS, 3 * CH), F32),
        jax.ShapeDtypeStruct((TOK, CH), F32),
        jax.ShapeDtypeStruct((1, CH), F32),
    )
    operands = [
        features[0], cotangent[0], long_filter, short_weight, skip_bias.reshape(1, CH),
        jnp.asarray(weights), jnp.asarray(inner), jnp.asarray(outer),
    ]
    operands = [pltpu.with_memory_space_constraint(operand, pltpu.HBM) for operand in operands]
    results = pl.pallas_call(
        kernel,
        out_shape=shapes,
        in_specs=[hbm] * 8,
        out_specs=(vmem,) * 5,
        scratch_shapes=[
            pltpu.VMEM((TOK, 3 * CH), BF16),
            pltpu.VMEM((TOK, CH), BF16),
            pltpu.VMEM((TOK, CH), F32),
            pltpu.VMEM((TAPS, 3 * CH), F32),
            pltpu.VMEM((1, CH), F32),
            pltpu.VMEM(weights.shape, BF16),
            pltpu.VMEM(inner.shape, F32),
            pltpu.VMEM(outer.shape, F32),
            pltpu.VMEM((2, CTX, 2 * GRP, TOK), BF16),
            pltpu.VMEM((2, CTX, 2 * GRP, TOK), BF16),
            pltpu.VMEM(block, F32),
            pltpu.VMEM((4, GRP, TOK), F32),
            pltpu.VMEM((DP, 4, GRP, TOK), F32),
            pltpu.VMEM((2, CTX, 2 * GRP, TOK), BF16),
            pltpu.VMEM((2, CTX, 2 * GRP, TOK), BF16),
            pltpu.VMEM((DP, 4, GRP, TOK), F32),
            pltpu.VMEM((DP, 4, GRP, TOK), F32),
            pltpu.VMEM((4, GRP, TOK), F32),
            pltpu.VMEM((4, GRP, TOK), F32),
            pltpu.VMEM((DP, 4, GRP, TOK), F32),
            pltpu.VMEM((4, 24, TOK), F32),
            pltpu.VMEM((TOK, TOK), F32),
            pltpu.VMEM((24, GRP, TOK), F32),
            pltpu.VMEM(block, F32),
            pltpu.VMEM(block, F32),
            pltpu.VMEM(block, F32),
            pltpu.VMEM(block, F32),
            pltpu.VMEM(block, F32),
            pltpu.VMEM(block, F32),
            pltpu.VMEM(block, F32),
            pltpu.VMEM((4, 8, 2, GRP, TOK), F32),
            pltpu.VMEM((CTX, GRP, 4 * TOK), BF16),
            pltpu.VMEM((CTX, GRP, 2 * TOK), F32),
            pltpu.VMEM((CTX, GRP, 2 * TOK), F32),
            pltpu.VMEM((CTX, GRP, 2 * TOK), F32),
            pltpu.VMEM((CTX, GRP, 2 * TOK), F32),
            pltpu.VMEM((2, 8, TOK), F32),
            pltpu.VMEM((DP, 8, TOK), F32),
            pltpu.VMEM((CTX, 8, TOK), F32),
            pltpu.SemaphoreType.DMA((12,)),
            pltpu.SemaphoreType.DMA((12,)),
            pltpu.SemaphoreType.DMA((8,)),
        ],
        compiler_params=pltpu.CompilerParams(
            collective_id=0, has_side_effects=True, vmem_limit_bytes=40 << 20
        ),
        name="hyena",
    )(*operands)
    out, gfeat, gshort, gfilt, gskip = pl.pallas_call(
        deliver,
        out_shape=shapes,
        in_specs=[vmem] * 5,
        out_specs=(hbm,) * 5,
        scratch_shapes=[pltpu.SemaphoreType.DMA((5,))],
        compiler_params=pltpu.CompilerParams(vmem_limit_bytes=4 << 20),
        name="deliver",
    )(*results)
    return (out[None], gfeat[None], gshort, gfilt, gskip.reshape(CH))


def solution(mesh):
    return jax.shard_map(
        per_device,
        mesh=mesh,
        in_specs=(P("dp", "ctx", None), P(), P("ctx", None), P(), P("dp", "ctx", None)),
        out_specs=(P("dp", "ctx", None), P("dp", "ctx", None), P(), P("ctx", None), P()),
        check_vma=False,
    )
```
